256 devices in a mesh: member: 4 (over x), region: 16 (over z, core), block: 4 (over y).
Axes of the slice: x: 4, y: 4, z: 8, core: 2. Of those that a mesh axis runs over, the one named last changes fastest.
Arguments:
- traffic_load: float32 [128, 524288], P('member', ('region', 'block')), may hold values from 0.05 to 0.7
- free_speed: float32 [524288], P(('region', 'block')), may hold values from 0.3 to 0.95
- wave_speed: float32 [524288], P(('region', 'block')), may hold values from 0.15 to 0.6
- jam_density: float32 [524288], P(('region', 'block')), may hold values from 0.8 to 1.2
- capacity_share: float32 [524288], P(('region', 'block')), may hold values from 0.5 to 1
- observation_cell: int32 [196608], P(('region', 'block')), may hold values from 0 to 2047
- obs_count: int32 [256], P(('region', 'block')), may hold values from 1 to 768, 98304 in all
- observation_value: float32 [196608], P(('region', 'block')), may hold values from 0 to 0.8
- observation_variance: float32 [196608], P(('region', 'block')), may hold values from 0.002 to 0.02
- observation_noise: float32 [128, 196608], P('member', ('region', 'block')), may hold values from -6 to 6
- block_lists: int32 [256, 3], P(('region', 'block')), may hold values from 0 to 255, as said below
Outputs:
- analysis: float32 [128, 524288], P('member', ('region', 'block'))
The draws below stay inside these ranges and needn't reach their ends.
Inputs may be any that keep to these rules, and one draw needn't show every extreme that they name: `block_lists`: row b lists 3 different blocks, b itself among them, each within 4 blocks of b.
All inputs are finite; a program needn't handle non-finite values. No bound on the sum of `obs_count` on one device may be relied on, other than what follows from the above.
Results may differ from the reference program's by a relative error of at most 0.0003.
Values sent between devices are 32-bit elements; how exact they have to be, the bound alone decides.
No kernel may reach another device: no remote copies, remote signals or barrier semaphores. Data moves between devices by JAX's collectives and lax.ppermute only.
A program may use at most 64 MiB of HBM per device.

```python
import math
import jax
import jax.numpy as jnp
import numpy as np
from jax import lax

REALIZATION_TALLY = 128
HORIZON_TICKS = 16
BLK_DEV = 4
NEIGH = 3
CELLS_PER_BLOCK = 2048
BLOCK_SLOTS = 768
NBLK = 256
NC = 524288
SLOT_COUNT = 196608


def draw_block_lists(key, part):
    reach_blocks = BLK_DEV
    span_count = 2 * reach_blocks + 1
    offsets = jnp.arange(span_count, dtype=jnp.int32) - reach_blocks
    owner_block = jnp.arange(NBLK, dtype=jnp.int32)[:, None]
    candidate = owner_block + offsets[None, :]
    usable = (candidate >= 0) & (candidate < NBLK)
    ranking = jax.random.randint(jax.random.fold_in(key, 17), (NBLK, span_count), 0, 1000, dtype=jnp.int32) * span_count + jnp.arange(span_count, dtype=jnp.int32)[None, :]
    ranking = jnp.where(usable, ranking, -1 - jnp.arange(span_count, dtype=jnp.int32)[None, :])
    ranking = jnp.where(offsets[None, :] == 0, 2000 * span_count, ranking)
    scores_top, chosen = lax.top_k(ranking, NEIGH)
    return jnp.take_along_axis(candidate, chosen, axis=1).astype(jnp.int32)


def set_ends(array, rng, low, top_value):
    extent = array.shape
    index_at = [jax.random.randint(jax.random.fold_in(rng, axis), (), 0, extent[axis]) for axis in range(len(extent))]
    array = array.at[tuple(index_at)].set(low)
    longest = extent.index(max(extent))
    index_at[longest] = (index_at[longest] + 1) % extent[longest]
    return array.at[tuple(index_at)].set(top_value)


def shard_levels(key, dims, shards, least, largest):
    level, own = 1.0, jax.random.fold_in(key, 6)
    for position, shards_of in shards:
        heights = jnp.exp(jax.random.uniform(jax.random.fold_in(own, position), (shards_of,), jnp.float32, least / len(shards), largest / len(shards)))
        level = level * jnp.repeat(heights, dims[position] // shards_of).reshape([-1 if axis == position else 1 for axis in range(len(dims))])
    return level


def split_up(number_of, total, most, skew):
    portions = [(1 << 20) // math.isqrt(standing ** skew) + 1 for standing in range(2, number_of + 1)]
    rest, given = total - most - (number_of - 1), [1] * (number_of - 1)
    while rest > 0:
        candidates = [i for i in range(number_of - 1) if given[i] < most]
        mass, budget = sum([portions[i] for i in candidates]), rest
        for i in candidates:
            addition = min(most - given[i], max(1, budget * portions[i] // mass), rest)
            given[i] = given[i] + addition
            rest = rest - addition
    return np.array([most] + given)


def ragged_sizes(key, number_of, total, bound, lean):
    if number_of == 2:
        one = jax.random.randint(key, (), max(1, total - bound), min(bound, total - 1) + 1)
        return jnp.stack([one, total - one])
    sizes = jnp.asarray(split_up(number_of, total, bound, lean), jnp.int32)
    couples = (number_of - 1) // 2
    donor, taker = sizes[1:1 + 2 * couples:2], sizes[2:2 + 2 * couples:2]
    room = jnp.minimum(donor - 1, bound - taker)
    shifted = jax.random.randint(jax.random.fold_in(key, 1), (couples,), 0, 1 << 20) % (room + 1)
    sizes = sizes.at[1:1 + 2 * couples:2].set(donor - shifted).at[2:2 + 2 * couples:2].set(taker + shifted)
    return sizes[jax.random.permutation(jax.random.fold_in(key, 2), number_of)]


def normal_values(stream_key, dims, width, most, cuts=(), kind=jnp.bfloat16):
    entries = width * jax.random.normal(stream_key, dims, jnp.float32)
    if cuts:
        entries = entries * shard_levels(stream_key, dims, cuts, -0.22, 0.18)
    return jnp.clip(entries, -most, most).astype(kind)


def setup_inputs(seed: int = 0) -> dict:
    seeds = jax.random.split(jax.random.key(seed), 12)
    return {
        "traffic_load": jnp.clip(0.05 + 0.65 * jax.random.uniform(seeds[0], (REALIZATION_TALLY, NC), jnp.float32) ** shard_levels(seeds[0], (REALIZATION_TALLY, NC), ((0, 4), (1, 64)), -0.2, 0.2), 0.05, 0.7),
        "free_speed": jnp.clip(jnp.exp(math.log(0.95) - 1.1526795 * jax.random.uniform(seeds[1], (NC,), jnp.float32) ** shard_levels(seeds[1], (NC,), ((0, 64),), -0.2, 0.2)), 0.3, 0.95),
        "wave_speed": jnp.clip(jnp.exp(math.log(0.6) - 1.3862944 * jax.random.uniform(seeds[2], (NC,), jnp.float32) ** shard_levels(seeds[2], (NC,), ((0, 64),), -0.2, 0.2)), 0.15, 0.6),
        "jam_density": jnp.clip(0.8 + 0.40000004 * jax.random.uniform(seeds[3], (NC,), jnp.float32) ** shard_levels(seeds[3], (NC,), ((0, 64),), -0.2, 0.2), 0.8, 1.2),
        "capacity_share": jnp.clip(0.5 + 0.5 * jax.random.uniform(seeds[4], (NC,), jnp.float32) ** shard_levels(seeds[4], (NC,), ((0, 64),), -0.2, 0.2), 0.5, 1.0),
        "observation_cell": set_ends(jax.random.randint(seeds[5], (SLOT_COUNT,), 0, CELLS_PER_BLOCK), jax.random.fold_in(seeds[5], 1), 0, CELLS_PER_BLOCK - 1).astype(jnp.int32),
        "obs_count": ragged_sizes(seeds[6], NBLK, NBLK * BLOCK_SLOTS // 2, BLOCK_SLOTS, 2).astype(jnp.int32),
        "observation_value": jnp.clip(0.8 * jax.random.uniform(seeds[7], (SLOT_COUNT,), jnp.float32) ** shard_levels(seeds[7], (SLOT_COUNT,), ((0, 64),), -0.2, 0.2), 0.0, 0.8),
        "observation_variance": jnp.clip(jnp.exp(math.log(0.02) - 2.30258502 * jax.random.uniform(seeds[8], (SLOT_COUNT,), jnp.float32) ** shard_levels(seeds[8], (SLOT_COUNT,), ((0, 64),), -0.2, 0.2)), 0.002, 0.02),
        "observation_noise": normal_values(seeds[9], (REALIZATION_TALLY, SLOT_COUNT), 1.0, 6.0, ((0, 4), (1, 64)), jnp.float32),
        "block_lists": draw_block_lists(jax.random.fold_in(seeds[11], 71), 0),
    }


def road_capacity(free_speed, wave_speed, jam_density, capacity_share):
    return capacity_share * free_speed * wave_speed * jam_density / (free_speed + wave_speed)

def block_products(left_side, right_side, weight, block_total):
    member_count = left_side.shape[0]
    left_blocks = (left_side * weight).reshape(member_count, block_total, -1)
    right_blocks = right_side.reshape(member_count, block_total, -1)
    return jnp.einsum('kbo,jbo->bkj', left_blocks, right_blocks, precision=lax.Precision.HIGHEST)

def reference(traffic_load, free_speed, wave_speed, jam_density, capacity_share, observation_cell, obs_count, observation_value, observation_variance, observation_noise, block_lists):
    capacity = road_capacity(free_speed, wave_speed, jam_density, capacity_share)
    member_count = traffic_load.shape[0]

    def propagate_traffic_load(step_index, state):
        demand = jnp.minimum(free_speed * state, capacity)
        supply = jnp.minimum(capacity, wave_speed * (jam_density - state))
        upstream = jnp.concatenate([jnp.zeros((member_count, 1), demand.dtype), demand], axis=1)
        exit_column = jnp.broadcast_to(capacity[-1:][None, :], (member_count, 1)).astype(supply.dtype)
        downstream = jnp.concatenate([supply, exit_column], axis=1)
        fluxes = jnp.minimum(upstream, downstream)
        return state + fluxes[:, :-1] - fluxes[:, 1:]
    predicted_traffic_load = lax.fori_loop(0, HORIZON_TICKS, propagate_traffic_load, traffic_load)
    realization_average = lax.optimization_barrier(jnp.sum(predicted_traffic_load, axis=0)) / REALIZATION_TALLY
    realization_departure = predicted_traffic_load - realization_average
    slot_cell_index = jnp.arange(SLOT_COUNT, dtype=jnp.int32) // BLOCK_SLOTS * CELLS_PER_BLOCK + observation_cell.astype(jnp.int32)
    obs_anomaly = jnp.take(realization_departure, slot_cell_index, axis=1)
    obs_mean = jnp.take(realization_average, slot_cell_index)
    live_mask = (jnp.arange(BLOCK_SLOTS, dtype=jnp.int32)[None, :] < obs_count[:, None]).reshape(-1).astype(observation_variance.dtype)
    weight = live_mask / observation_variance
    misfit = observation_value - obs_mean
    spread = lax.optimization_barrier(jnp.sum(obs_anomaly * obs_anomaly, axis=0)) / (REALIZATION_TALLY - 1)
    misfit_sum = jnp.sum(misfit * misfit * weight)
    spread_sum = jnp.sum(live_mask * (spread / observation_variance + 1.0))
    inflation = jnp.sqrt(misfit_sum / spread_sum)
    perturbed = misfit + jnp.sqrt(observation_variance) * observation_noise
    gram_part = block_products(obs_anomaly, obs_anomaly, weight, NBLK)
    cross_part = block_products(obs_anomaly, perturbed, weight, NBLK)
    local_gram = gram_part[block_lists[:, 0]]
    local_cross = cross_part[block_lists[:, 0]]
    for entry in range(1, NEIGH):
        local_gram = local_gram + gram_part[block_lists[:, entry]]
        local_cross = local_cross + cross_part[block_lists[:, entry]]
    system = (REALIZATION_TALLY - 1) * jnp.eye(REALIZATION_TALLY, dtype=local_gram.dtype)[None] + inflation * inflation * local_gram
    right_side = inflation * local_cross - inflation * inflation * local_gram
    mixing = jnp.linalg.solve(system, right_side)
    anomaly_blocks = realization_departure.reshape(member_count, NBLK, CELLS_PER_BLOCK)
    change = jnp.einsum('kbc,bkj->jbc', anomaly_blocks, mixing, precision=lax.Precision.HIGHEST).reshape(member_count, NC)
    return realization_average + inflation * realization_departure + inflation * change
```

```python
import jax
import jax.numpy as jnp
from jax import lax
from jax.experimental import pallas as pl
from jax.experimental.pallas import tpu as pltpu
from jax.sharding import PartitionSpec as P

TALLY = 128
TICKS = 16
CELLS = 2048
SLOTS = 768
LANES = 128
RB = ("region", "block")
HIGHEST = lax.Precision.HIGHEST


def vmem(n):
    return [pl.BlockSpec(memory_space=pltpu.VMEM) for _ in range(n)]


def forecast_kernel(state_ref, low_ref, high_ref, road_ref, cell_ref, fore_ref, obs_ref, wide_ref, side_ref):
    rows, width = state_ref.shape
    full = width + 2 * LANES
    wide_ref[:, :LANES] = low_ref[:rows, :]
    wide_ref[:, LANES : LANES + width] = state_ref[...]
    wide_ref[:, LANES + width :] = high_ref[:rows, :]
    side_ref[0:4, :LANES] = low_ref[rows : rows + 4, :]
    side_ref[0:4, LANES : LANES + width] = road_ref[...]
    side_ref[0:4, LANES + width :] = high_ref[rows : rows + 4, :]

    def step(_, carry):
        for g in range(rows // 8):
            at = pl.ds(8 * g, 8)
            x = wide_ref[at, :]
            speed = side_ref[0:1, :]
            wave = side_ref[1:2, :]
            jam = side_ref[2:3, :]
            cap = side_ref[3:4, :]
            demand = jnp.minimum(speed * x, cap)
            supply = jnp.minimum(cap, wave * (jam - x))
            flux = jnp.minimum(demand, pltpu.roll(supply, full - 1, 1))
            wide_ref[at, :] = x + pltpu.roll(flux, 1, 1) - flux
        return carry

    lax.fori_loop(0, TICKS, step, 0)
    blocks = width // CELLS
    for b in range(blocks):
        fore_ref[b] = wide_ref[:, LANES + b * CELLS : LANES + (b + 1) * CELLS]

    def gather(q, carry):
        b = q // (SLOTS // LANES)
        cells = cell_ref[pl.ds(q, 1), :]
        lane = jnp.broadcast_to(cells & (LANES - 1), (8, LANES))
        tile = jnp.broadcast_to(cells >> 7, (8, LANES))
        acc = [jnp.zeros((8, LANES), jnp.float32) for _ in range(rows // 8)]
        for c in range(CELLS // LANES):
            hit = tile == c
            for g in range(rows // 8):
                piece = fore_ref[b, pl.ds(8 * g, 8), c * LANES : (c + 1) * LANES]
                got = jnp.take_along_axis(piece, lane, axis=1)
                acc[g] = jnp.where(hit, got, acc[g])
        for g in range(rows // 8):
            obs_ref[q, pl.ds(8 * g, 8), :] = acc[g]
        return carry

    lax.fori_loop(0, blocks * (SLOTS // LANES), gather, 0)


def forecast(state, low, high, road, cells):
    rows, width = state.shape
    blocks = width // CELLS
    chunks = blocks * SLOTS // LANES
    return pl.pallas_call(
        forecast_kernel,
        out_shape=(
            jax.ShapeDtypeStruct((blocks, rows, CELLS), jnp.float32),
            jax.ShapeDtypeStruct((chunks, rows, LANES), jnp.float32),
        ),
        in_specs=vmem(5),
        out_specs=tuple(vmem(2)),
        scratch_shapes=[
            pltpu.VMEM((rows, width + 2 * LANES), jnp.float32),
            pltpu.VMEM((8, width + 2 * LANES), jnp.float32),
        ],
        name="forecast",
    )(state, low, high, road, cells)


def products_kernel(obs_ref, noise_ref, slot_ref, count_ref, pair_ref, sum_ref):
    chunks = obs_ref.shape[1]
    pieces = [jnp.concatenate([obs_ref[m, q] for m in range(obs_ref.shape[0])], axis=0) for q in range(chunks)]
    noises = [jnp.concatenate([noise_ref[m, q] for m in range(noise_ref.shape[0])], axis=0) for q in range(chunks)]
    count = count_ref[0, 0]
    total_a = jnp.zeros((1, LANES), jnp.float32)
    total_b = jnp.zeros((1, LANES), jnp.float32)
    scaled, plain, moved = [], [], []
    for q in range(chunks):
        x = pieces[q]
        value = slot_ref[0, pl.ds(q, 1), :]
        variance = slot_ref[1, pl.ds(q, 1), :]
        mean = jnp.sum(x, axis=0, keepdims=True) / TALLY
        a = x - mean
        slot = lax.broadcasted_iota(jnp.int32, (1, LANES), 1) + q * LANES
        live = (slot < count).astype(jnp.float32)
        weight = live / variance
        misfit = value - mean
        spread = jnp.sum(a * a, axis=0, keepdims=True) / (TALLY - 1)
        total_a += misfit * misfit * weight
        total_b += live * (spread / variance + 1.0)
        scaled.append(a * weight)
        plain.append(a)
        moved.append(misfit + jnp.sqrt(variance) * noises[q])
    left = jnp.concatenate(scaled, axis=1)
    dims = (((1,), (1,)), ((), ()))
    pair_ref[0] = lax.dot_general(left, jnp.concatenate(plain, axis=1), dims, precision=HIGHEST, preferred_element_type=jnp.float32)
    pair_ref[1] = lax.dot_general(left, jnp.concatenate(moved, axis=1), dims, precision=HIGHEST, preferred_element_type=jnp.float32)
    row = lax.broadcasted_iota(jnp.int32, (8, LANES), 0)
    sum_a = jnp.sum(total_a, axis=1, keepdims=True)
    sum_b = jnp.sum(total_b, axis=1, keepdims=True)
    sum_ref[...] = jnp.where(row == 0, sum_a, jnp.where(row == 1, sum_b, 0.0))


def products(obs, noise, slots, count):
    return pl.pallas_call(
        products_kernel,
        out_shape=(
            jax.ShapeDtypeStruct((2, TALLY, TALLY), jnp.float32),
            jax.ShapeDtypeStruct((8, LANES), jnp.float32),
        ),
        in_specs=vmem(3) + [pl.BlockSpec(memory_space=pltpu.SMEM)],
        out_specs=tuple(vmem(2)),
        name="products",
    )(obs, noise, slots, count)


def solve_kernel(part_ref, sums_ref, mixing_ref, scale_ref):
    sums = jnp.sum(sums_ref[...], axis=0)
    scale = jnp.sqrt(sums[0:1, :] / sums[1:2, :])
    scale_ref[...] = jnp.broadcast_to(scale, (8, LANES))
    gram = part_ref[0, 0]
    cross = part_ref[0, 1]
    for m in range(1, part_ref.shape[0]):
        gram = gram + part_ref[m, 0]
        cross = cross + part_ref[m, 1]
    row = lax.broadcasted_iota(jnp.int32, (TALLY, TALLY), 0)
    lane = lax.broadcasted_iota(jnp.int32, (TALLY, TALLY), 1)
    eye = jnp.where(row == lane, jnp.float32(TALLY - 1), jnp.float32(0.0))
    system = eye + (scale * scale) * gram
    target = eye + scale * cross
    both = jnp.concatenate([system, target], axis=1)
    tiles = [both[8 * i : 8 * i + 8, :] for i in range(TALLY // 8)]
    sub = lax.broadcasted_iota(jnp.int32, (8, 2 * TALLY), 0)
    for k in range(TALLY // 8):
        panel = tiles[k]
        for j in range(8):
            at = 8 * k + j
            column = panel[:, at : at + 1]
            pivot_row = panel[j : j + 1, :]
            inverse = 1.0 / panel[j : j + 1, at : at + 1]
            pivot_row = pivot_row * inverse
            panel = jnp.where(sub == j, pivot_row, panel - column * pivot_row)
        for i in range(TALLY // 8):
            if i != k:
                tile = tiles[i]
                new = tile
                for j in range(8):
                    new = new - tile[:, 8 * k + j : 8 * k + j + 1] * panel[j : j + 1, :]
                tiles[i] = new
        tiles[k] = panel
    for i in range(TALLY // 8):
        mixing_ref[8 * i : 8 * i + 8, :] = tiles[i][:, TALLY:]


def solve(parts, sums):
    return pl.pallas_call(
        solve_kernel,
        out_shape=(
            jax.ShapeDtypeStruct((TALLY, TALLY), jnp.float32),
            jax.ShapeDtypeStruct((8, LANES), jnp.float32),
        ),
        in_specs=vmem(2),
        out_specs=tuple(vmem(2)),
        name="solve",
    )(parts, sums)


def analysis_kernel(fore_ref, mixing_ref, scale_ref, out_ref):
    groups = fore_ref.shape[0]
    state = jnp.concatenate([fore_ref[m] for m in range(groups)], axis=0)
    mean = jnp.sum(state, axis=0, keepdims=True) / TALLY
    anomaly = state - mean
    mixing = mixing_ref[...] * scale_ref[0:1, :]
    change = lax.dot_general(
        mixing, anomaly, (((0,), (0,)), ((), ())), precision=HIGHEST, preferred_element_type=jnp.float32
    )
    out = mean + change
    rows = fore_ref.shape[1]
    for m in range(groups):
        out_ref[m] = out[m * rows : (m + 1) * rows, :]


def analysis(fore, mixing, scale):
    return pl.pallas_call(
        analysis_kernel,
        out_shape=jax.ShapeDtypeStruct(fore.shape, jnp.float32),
        in_specs=vmem(3),
        out_specs=vmem(1)[0],
        name="analysis",
    )(fore, mixing, scale)


def shared_sums(value, axes):
    size = 1
    for axis in axes:
        size *= lax.axis_size(axis)
    copies = jnp.broadcast_to(value[None], (size,) + value.shape)
    return lax.all_to_all(copies, axes, 0, 0)


def body(load, free_speed, wave_speed, jam_density, capacity_share, cell, count, value, variance, noise, lists):
    rows, width = load.shape
    blocks = width // CELLS
    members = lax.axis_size("member")
    member = lax.axis_index("member")
    slab = lax.axis_index(RB)
    slabs = lax.axis_size(RB)
    up = [(i, i + 1) for i in range(slabs - 1)]
    down = [(b, a) for a, b in up]

    capacity = capacity_share * free_speed * wave_speed * jam_density / (free_speed + wave_speed)
    road = jnp.stack([free_speed, wave_speed, jam_density, capacity])
    edge_last = jnp.concatenate([load[:, width - TICKS :], road[:, width - TICKS :]], axis=0)
    edge_first = jnp.concatenate([load[:, :TICKS], road[:, :TICKS]], axis=0)
    low = lax.ppermute(edge_last, RB, up)
    high = lax.ppermute(edge_first, RB, down)
    beyond = jnp.concatenate(
        [jnp.zeros((rows + 1,)), jnp.array([1.0, 1000.0]), capacity[width - 1 :]]
    ).astype(jnp.float32)
    high = jnp.where(slab == slabs - 1, beyond[:, None], high)
    low = jnp.pad(low, ((0, 0), (LANES - TICKS, 0)))
    high = jnp.pad(high, ((0, 0), (0, LANES - TICKS)))

    per_block = SLOTS // LANES
    noise_out = noise.reshape(rows, blocks * per_block, LANES).transpose(1, 0, 2).reshape(blocks, per_block, rows, LANES)
    noise_all = lax.all_to_all(noise_out, "member", 0, 0)
    fore, obs = forecast(load, low, high, road, cell.reshape(blocks * per_block, LANES))
    obs_all = lax.all_to_all(obs.reshape(blocks, per_block, rows, LANES), "member", 0, 0)
    fore_all = lax.all_to_all(fore, "member", 0, 0)

    slots = jnp.stack([value, variance]).reshape(2, blocks, per_block, LANES)
    slots = lax.dynamic_index_in_dim(slots, member, 1, keepdims=False)
    own_count = lax.dynamic_slice_in_dim(count, member, 1).reshape(1, 1)
    pair, sums = products(obs_all, noise_all, slots, own_count)

    below = lax.ppermute(pair, RB, up)
    above = lax.ppermute(pair, RB, down)
    sums = jnp.sum(shared_sums(sums, ("member", "block")), axis=0)
    sums = shared_sums(sums, ("region",))

    names = (slab + jnp.arange(-1, 2, dtype=jnp.int32)) * blocks + member
    chosen = jnp.any(lists[:, None, :] == names[None, :, None], axis=2)
    chosen = chosen.astype(jnp.float32)[:, :, None, None, None]
    parts = chosen[:, 0] * below[None] + chosen[:, 1] * pair[None] + chosen[:, 2] * above[None]
    parts = lax.all_to_all(parts, "member", 0, 0)
    mixing, scale = solve(parts, sums)
    out = analysis(fore_all, mixing, scale)
    out = lax.all_to_all(out, "member", 0, 0)
    return out.transpose(1, 0, 2).reshape(rows, width)


def solution(mesh):
    in_specs = (
        P("member", RB), P(RB), P(RB), P(RB), P(RB), P(RB), P(RB), P(RB), P(RB), P("member", RB), P(RB, None),
    )
    return jax.shard_map(body, mesh=mesh, in_specs=in_specs, out_specs=P("member", RB), check_vma=False)
```

```python
import jax
import jax.numpy as jnp
from jax import lax
from jax.experimental import pallas as pl
from jax.experimental.pallas import tpu as pltpu
from jax.sharding import PartitionSpec as P

TALLY = 128
TICKS = 16
CELLS = 2048
SLOTS = 768
LANES = 128
GROUP = 4
PER_BLOCK = SLOTS // LANES
RB = ("region", "block")
ALL = ("member", "region", "block")
HIGHEST = lax.Precision.HIGHEST
VMEM = pl.BlockSpec(memory_space=pltpu.VMEM)
SMEM = pl.BlockSpec(memory_space=pltpu.SMEM)
HBM = pl.BlockSpec(memory_space=pltpu.HBM)


def room(mib):
    return pltpu.CompilerParams(vmem_limit_bytes=mib << 20)


PAIR = jax.ShapeDtypeStruct((2, TALLY, TALLY), jnp.float32)


def road_capacity(free_speed, wave_speed, jam_density, capacity_share):
    return capacity_share * free_speed * wave_speed * jam_density / (free_speed + wave_speed)


def edges_kernel(place_ref, state_ref, speed_ref, wave_ref, jam_ref, share_ref, noise_ref, *refs):
    last_ref, first_ref = refs[:2]
    noise_refs = refs[2 : 2 + GROUP]
    tile_refs = refs[2 + GROUP : 4 + GROUP]
    sem_ref = refs[4 + GROUP]
    rows, width = state_ref.shape
    member = place_ref[0]
    copies = []
    for side, tile_ref in enumerate(tile_refs):
        at = pl.ds((1 - side) * (width - LANES), LANES)
        copies.append(pltpu.make_async_copy(state_ref.at[:, at], tile_ref.at[pl.ds(0, rows), :], sem_ref.at[side]))
        for i, road_ref in enumerate((speed_ref, wave_ref, jam_ref, share_ref)):
            copies.append(
                pltpu.make_async_copy(
                    road_ref.at[:, at], tile_ref.at[pl.ds(rows + i, 1), :], sem_ref.at[2 + 4 * side + i]
                )
            )
    for d in range(GROUP):
        at = pl.ds(pl.multiple_of(lax.rem(member + d, GROUP) * SLOTS, LANES), SLOTS)
        copies.append(pltpu.make_async_copy(noise_ref.at[:, at], noise_refs[d], sem_ref.at[10 + d]))
    for copy in copies:
        copy.start()
    for copy in copies:
        copy.wait()
    last_ref[...] = tile_refs[0][:, LANES - TICKS :]
    first_ref[...] = tile_refs[1][:, :TICKS]


def edges(place, state, road, noise):
    rows = state.shape[0]
    edge = jax.ShapeDtypeStruct((rows + 4, TICKS), jnp.float32)
    piece = jax.ShapeDtypeStruct((rows, SLOTS), jnp.float32)
    return pl.pallas_call(
        edges_kernel,
        out_shape=(edge,) * 2 + (piece,) * GROUP,
        in_specs=[SMEM] + [HBM] * 6,
        out_specs=(VMEM,) * (2 + GROUP),
        scratch_shapes=[pltpu.VMEM((rows + 4, LANES), jnp.float32)] * 2 + [pltpu.SemaphoreType.DMA((10 + GROUP,))],
        compiler_params=room(4),
        name="edges",
    )(place, state, *road, noise)


def forecast_kernel(
    place_ref, state_ref, low_ref, high_ref, speed_ref, wave_ref, jam_ref, share_ref, cells_ref, *refs
):
    fore_refs, obs_refs = refs[:GROUP], refs[GROUP : 2 * GROUP]
    wide_ref, other_ref, side_ref, share_at, cell_ref, sem_ref = refs[2 * GROUP :]
    rows, width = state_ref.shape
    full = width + 2 * LANES
    main = slice(LANES, LANES + width)
    inner = pl.ds(LANES, width)
    roads = [
        pltpu.make_async_copy(ref, side_ref.at[pl.ds(i, 1), inner], sem_ref.at[i])
        for i, ref in enumerate((speed_ref, wave_ref, jam_ref))
    ]
    roads.append(pltpu.make_async_copy(share_ref, share_at, sem_ref.at[3]))
    arrive = pltpu.make_async_copy(state_ref, wide_ref.at[:, inner], sem_ref.at[4])
    fetch = pltpu.make_async_copy(cells_ref, cell_ref, sem_ref.at[5])
    for copy in roads + [arrive, fetch]:
        copy.start()
    member = place_ref[0]
    slab = place_ref[1]
    is_first = slab == 0
    is_last = slab == place_ref[2] - 1
    for copy in roads:
        copy.wait()
    capacity = road_capacity(side_ref[0:1, main], side_ref[1:2, main], side_ref[2:3, main], share_at[...])
    side_ref[3:4, main] = capacity
    edge = jnp.zeros((rows + 4, LANES - TICKS), jnp.float32)
    low = jnp.concatenate([edge, low_ref[...]], axis=1)
    high = jnp.concatenate([high_ref[...], edge], axis=1)
    wide_ref[:, :LANES] = low[:rows]
    wide_ref[:, LANES + width :] = high[:rows]
    lane = lax.broadcasted_iota(jnp.int32, (1, LANES), 1)
    for piece, at, inside, beyond in (
        (low, slice(0, LANES), lane >= LANES - TICKS, is_first),
        (high, slice(LANES + width, full), lane < TICKS, is_last),
    ):
        inside = inside & jnp.logical_not(beyond)
        s, w, j, c = [piece[rows + i : rows + i + 1] for i in range(4)]
        s = jnp.where(inside, s, 1.0)
        w = jnp.where(inside, w, 1.0)
        j = jnp.where(inside, j, 1.0)
        c = jnp.where(inside, c, 0.0)
        side_ref[0:1, at] = s
        side_ref[1:2, at] = w
        side_ref[2:3, at] = j
        side_ref[3:4, at] = road_capacity(s, w, j, c)

    @pl.when(is_last)
    def _():
        at = slice(LANES + width, full)
        side_ref[0:1, at] = jnp.zeros((1, LANES), jnp.float32)
        side_ref[2:3, at] = jnp.full((1, LANES), 1000.0, jnp.float32)
        side_ref[3:4, at] = jnp.broadcast_to(capacity[:, width - 1 :], (1, LANES))

    arrive.wait()

    def half(src, dst):
        for g in range(rows // 8):
            at = slice(8 * g, 8 * g + 8)
            x = src[at, :]
            cap = side_ref[3:4, :]
            demand = jnp.minimum(side_ref[0:1, :] * x, cap)
            supply = jnp.minimum(cap, side_ref[1:2, :] * (side_ref[2:3, :] - x))
            flux = jnp.minimum(demand, pltpu.roll(supply, full - 1, 1))
            dst[at, :] = x + pltpu.roll(flux, 1, 1) - flux

    def step(_, carry):
        half(wide_ref, other_ref)
        half(other_ref, wide_ref)
        return carry

    lax.fori_loop(0, TICKS // 2, step, 0)
    starts = [pl.multiple_of(LANES + lax.rem(member + d, GROUP) * CELLS, LANES) for d in range(GROUP)]
    leave = [
        pltpu.make_async_copy(wide_ref.at[:, pl.ds(starts[d], CELLS)], fore_refs[d], sem_ref.at[6 + d])
        for d in range(GROUP)
    ]
    for copy in leave:
        copy.start()
    fetch.wait()
    for d, obs_ref in enumerate(obs_refs):
        b = lax.rem(member + d, GROUP)
        start = starts[d]

        def gather(q, carry):
            cells = cell_ref[pl.ds(b * PER_BLOCK + q, 1), :]
            at_lane = jnp.broadcast_to(cells & (LANES - 1), (8, LANES))
            tile = jnp.broadcast_to(cells >> 7, (8, LANES))
            acc = [jnp.zeros((8, LANES), jnp.float32) for _ in range(rows // 8)]
            for c in range(CELLS // LANES):
                hit = tile == c
                for g in range(rows // 8):
                    piece = wide_ref[8 * g : 8 * g + 8, pl.ds(start + c * LANES, LANES)]
                    acc[g] = jnp.where(hit, jnp.take_along_axis(piece, at_lane, axis=1), acc[g])
            for g in range(rows // 8):
                obs_ref[q, 8 * g : 8 * g + 8, :] = acc[g]
            return carry

        lax.fori_loop(0, PER_BLOCK, gather, 0, unroll=True)
    for copy in leave:
        copy.wait()


def forecast(place, state, low, high, road, cells):
    rows, width = state.shape
    piece = jax.ShapeDtypeStruct((PER_BLOCK, rows, LANES), jnp.float32)
    return pl.pallas_call(
        forecast_kernel,
        out_shape=(jax.ShapeDtypeStruct((rows, CELLS), jnp.float32),) * GROUP + (piece,) * GROUP,
        in_specs=[SMEM, HBM, VMEM, VMEM] + [HBM] * 5,
        out_specs=(HBM,) * GROUP + (VMEM,) * GROUP,
        scratch_shapes=[
            pltpu.VMEM((rows, width + 2 * LANES), jnp.float32),
            pltpu.VMEM((rows, width + 2 * LANES), jnp.float32),
            pltpu.VMEM((8, width + 2 * LANES), jnp.float32),
            pltpu.VMEM((1, width), jnp.float32),
            pltpu.VMEM(cells.shape, jnp.int32),
            pltpu.SemaphoreType.DMA((6 + GROUP,)),
        ],
        compiler_params=room(12),
        name="forecast",
    )(place, state, low, high, *road, cells)


def products_kernel(*refs):
    place_ref, counts_ref = refs[:2]
    obs_refs, noise_refs = refs[2 : 2 + GROUP], refs[2 + GROUP : 2 + 2 * GROUP]
    value_ref, variance_ref, pair_ref, sum_ref, obs_ref, noise_ref, count_ref, sem_ref = refs[2 + 2 * GROUP :]
    fetch = pltpu.make_async_copy(counts_ref, count_ref, sem_ref.at[0])
    fetch.start()
    member = place_ref[0]
    rows = noise_refs[0].shape[0]
    for d in range(GROUP):
        at = pl.multiple_of(lax.rem(member - d + GROUP, GROUP) * rows, rows)
        for q in range(PER_BLOCK):
            obs_ref[pl.ds(at, rows), q * LANES : (q + 1) * LANES] = obs_refs[d][q]
        noise_ref[pl.ds(at, rows), :] = noise_refs[d][...]
    fetch.wait()
    count = count_ref[member]
    total_a = jnp.zeros((1, LANES), jnp.float32)
    total_b = jnp.zeros((1, LANES), jnp.float32)
    scaled, plain, moved = [], [], []
    for q in range(PER_BLOCK):
        at = slice(q * LANES, (q + 1) * LANES)
        x = obs_ref[:, at]
        value = value_ref[pl.ds(member * PER_BLOCK + q, 1), :]
        variance = variance_ref[pl.ds(member * PER_BLOCK + q, 1), :]
        mean = jnp.sum(x, axis=0, keepdims=True) / TALLY
        a = x - mean
        slot = lax.broadcasted_iota(jnp.int32, (1, LANES), 1) + q * LANES
        live = (slot < count).astype(jnp.float32)
        weight = live / variance
        misfit = value - mean
        spread = jnp.sum(a * a, axis=0, keepdims=True) / (TALLY - 1)
        total_a += misfit * misfit * weight
        total_b += live * (spread / variance + 1.0)
        scaled.append(a * weight)
        plain.append(a)
        moved.append(misfit + jnp.sqrt(variance) * noise_ref[:, at])
    left = jnp.concatenate(scaled, axis=1)
    right = jnp.concatenate([jnp.concatenate(plain, axis=1), jnp.concatenate(moved, axis=1)], axis=0)
    dims = (((1,), (1,)), ((), ()))
    both = lax.dot_general(left, right, dims, precision=HIGHEST, preferred_element_type=jnp.float32)
    pair_ref[0] = both[:, :TALLY]
    pair_ref[1] = both[:, TALLY:]
    lane = lax.broadcasted_iota(jnp.int32, (1, LANES), 1)
    sum_a = jnp.sum(total_a, axis=1, keepdims=True)
    sum_b = jnp.sum(total_b, axis=1, keepdims=True)
    sums = jnp.where(lane == 0, sum_a, jnp.where(lane == 1, sum_b, 0.0))
    sum_ref[...] = jnp.broadcast_to(sums[None], sum_ref.shape)


def products(place, count, obs, noise, value, variance, devices):
    rows = noise[0].shape[0]
    return pl.pallas_call(
        products_kernel,
        out_shape=(PAIR, jax.ShapeDtypeStruct((devices, 1, LANES), jnp.float32)),
        in_specs=[SMEM, HBM] + [VMEM] * (2 * GROUP + 2),
        out_specs=(VMEM, VMEM),
        scratch_shapes=[pltpu.VMEM((GROUP * rows, SLOTS), jnp.float32)] * 2
        + [pltpu.SMEM((GROUP,), jnp.int32), pltpu.SemaphoreType.DMA((1,))],
        compiler_params=room(6),
        name="products",
    )(place, count, *obs, *noise, value, variance)


def select_kernel(place_ref, list_ref, below_ref, pair_ref, above_ref, *out_refs):
    member = place_ref[0]
    slab = place_ref[1]
    for d in range(GROUP):
        target = lax.rem(member + d, GROUP)
        total = None
        for step, ref in ((0, pair_ref), (-1, below_ref), (1, above_ref)):
            name = (slab + step) * GROUP + member
            listed = (list_ref[target, 0] == name) | (list_ref[target, 1] == name) | (list_ref[target, 2] == name)
            share = jnp.where(listed, jnp.float32(1.0), jnp.float32(0.0)) * ref[...]
            total = share if total is None else total + share
        out_refs[d][...] = total


def select(place, lists, below, pair, above):
    return pl.pallas_call(
        select_kernel,
        out_shape=(PAIR,) * GROUP,
        in_specs=[SMEM, SMEM] + [VMEM] * 3,
        out_specs=(VMEM,) * GROUP,
        compiler_params=room(6),
        name="select",
    )(place, lists, below, pair, above)


def update_kernel(place_ref, part0_ref, part1_ref, part2_ref, part3_ref, sums_ref, *refs):
    fore_refs = refs[:GROUP]
    out_ref, state_ref, sem_ref = refs[GROUP:]
    rows = fore_refs[0].shape[0]
    member = place_ref[0]
    arrive = []
    for d in range(GROUP):
        at = pl.multiple_of(lax.rem(member - d + GROUP, GROUP) * rows, rows)
        arrive.append(pltpu.make_async_copy(fore_refs[d], state_ref.at[pl.ds(at, rows), :], sem_ref.at[d]))
    for copy in arrive:
        copy.start()
    sums = jnp.sum(sums_ref[...], axis=0, keepdims=True)
    scale = jnp.sqrt(sums[:, 0:1] / sums[:, 1:2])
    gram = (part0_ref[0] + part1_ref[0]) + (part2_ref[0] + part3_ref[0])
    cross = (part0_ref[1] + part1_ref[1]) + (part2_ref[1] + part3_ref[1])
    row = lax.broadcasted_iota(jnp.int32, (TALLY, TALLY), 0)
    lane = lax.broadcasted_iota(jnp.int32, (TALLY, TALLY), 1)
    eye = jnp.where(row == lane, jnp.float32(TALLY - 1), jnp.float32(0.0))
    both = jnp.concatenate([eye + (scale * scale) * gram, eye + scale * cross], axis=1)
    tiles = [both[8 * i : 8 * i + 8, :] for i in range(TALLY // 8)]
    sub = lax.broadcasted_iota(jnp.int32, (8, 2 * TALLY), 0)
    for k in range(TALLY // 8):
        panel = tiles[k]
        for j in range(8):
            at = 8 * k + j
            column = panel[:, at : at + 1]
            pivot_row = panel[j : j + 1, :]
            inverse = 1.0 / panel[j : j + 1, at : at + 1]
            pivot_row = pivot_row * inverse
            panel = jnp.where(sub == j, pivot_row, panel - column * pivot_row)
        for i in range(TALLY // 8):
            if i != k:
                tile = tiles[i]
                new = tile
                for j in range(8):
                    new = new - tile[:, 8 * k + j : 8 * k + j + 1] * panel[j : j + 1, :]
                tiles[i] = new
        tiles[k] = panel
    mixing = jnp.concatenate([tile[:, TALLY:] for tile in tiles], axis=0) * scale
    for copy in arrive:
        copy.wait()
    state = state_ref[...]
    mean = jnp.sum(state, axis=0, keepdims=True) / TALLY
    anomaly = state - mean
    dims = (((0,), (0,)), ((), ()))
    out = mean + lax.dot_general(mixing, anomaly, dims, precision=HIGHEST, preferred_element_type=jnp.float32)
    for m in range(GROUP):
        out_ref[m] = out[m * rows : (m + 1) * rows, :]


def update(place, parts, sums, fore):
    return pl.pallas_call(
        update_kernel,
        out_shape=jax.ShapeDtypeStruct((GROUP,) + fore[0].shape, jnp.float32),
        in_specs=[SMEM] + [VMEM] * 5 + [HBM] * GROUP,
        out_specs=VMEM,
        scratch_shapes=[pltpu.VMEM((TALLY, CELLS), jnp.float32), pltpu.SemaphoreType.DMA((GROUP,))],
        compiler_params=room(10),
        name="update",
    )(place, *parts, sums, *fore)


def hold(value):
    return pltpu.with_memory_space_constraint(value, pltpu.HBM)


def exchange(pieces):
    moved = {
        d: lax.ppermute(pieces[d], "member", [(i, (i + d) % GROUP) for i in range(GROUP)]) for d in (2, 1, 3)
    }
    return [pieces[0], moved[1], moved[2], moved[3]]


def body(load, free_speed, wave_speed, jam_density, capacity_share, cell, count, value, variance, noise, lists):
    rows, width = load.shape
    member = lax.axis_index("member")
    slab = lax.axis_index(RB)
    slabs = lax.axis_size(RB)
    up = [(i, i + 1) for i in range(slabs - 1)]
    down = [(b, a) for a, b in up]
    place = jnp.stack([member, slab, jnp.int32(slabs)]).astype(jnp.int32)

    road = [hold(v.reshape(1, width)) for v in (free_speed, wave_speed, jam_density, capacity_share)]
    load, noise, count, cells = [hold(v) for v in (load, noise, count, cell.reshape(-1, LANES))]
    last, first, *noises = edges(place, load, road, noise)
    low = lax.ppermute(last, RB, up)
    high = lax.ppermute(first, RB, down)
    out = forecast(place, load, low, high, road, cells)
    fore, obs = out[:GROUP], out[GROUP:]
    obs = exchange(obs)
    noises = exchange(noises)
    fore = exchange(fore)

    pair, sums = products(
        place, count, obs, noises, value.reshape(-1, LANES), variance.reshape(-1, LANES), GROUP * slabs
    )
    below = lax.ppermute(pair, RB, up)
    above = lax.ppermute(pair, RB, down)
    below, above, sums = lax.optimization_barrier((below, above, sums))
    sums = lax.all_to_all(sums, ALL, 0, 0).reshape(GROUP * slabs, LANES)
    parts = exchange(select(place, lists, below, pair, above))
    out = update(place, parts, sums, fore)
    out = lax.all_to_all(out, "member", 0, 0)
    return out.transpose(1, 0, 2).reshape(rows, width)


def solution(mesh):
    slab = P(RB)
    in_specs = (P("member", RB),) + (slab,) * 8 + (P("member", RB), P(RB, None))
    return jax.shard_map(body, mesh=mesh, in_specs=in_specs, out_specs=P("member", RB), check_vma=False)
```

```python
import jax
import jax.numpy as jnp
from jax import lax
from jax.experimental import pallas as pl
from jax.experimental.pallas import tpu as pltpu
from jax.sharding import PartitionSpec as P

TALLY = 128
TICKS = 16
CELLS = 2048
SLOTS = 768
LANES = 128
GROUP = 4
PER_BLOCK = SLOTS // LANES
RB = ("region", "block")
ALL = ("member", "region", "block")
HIGHEST = lax.Precision.HIGHEST
VMEM = pl.BlockSpec(memory_space=pltpu.VMEM)
SMEM = pl.BlockSpec(memory_space=pltpu.SMEM)
HBM = pl.BlockSpec(memory_space=pltpu.HBM)


def room(mib):
    return pltpu.CompilerParams(vmem_limit_bytes=mib << 20)


PAIR = jax.ShapeDtypeStruct((2, TALLY, TALLY), jnp.float32)


def road_capacity(free_speed, wave_speed, jam_density, capacity_share):
    return capacity_share * free_speed * wave_speed * jam_density / (free_speed + wave_speed)


def edges_kernel(place_ref, state_ref, speed_ref, wave_ref, jam_ref, share_ref, noise_ref, *refs):
    near_ref, far_ref = refs[:2]
    noise_refs = refs[2 : 2 + GROUP]
    tile_refs = refs[2 + GROUP : 4 + GROUP]
    sem_ref = refs[4 + GROUP]
    rows, width = state_ref.shape
    member = place_ref[0]
    copies = []
    for side, tile_ref in enumerate(tile_refs):
        at = pl.ds((1 - side) * (width - LANES), LANES)
        copies.append(pltpu.make_async_copy(state_ref.at[:, at], tile_ref.at[pl.ds(0, rows), :], sem_ref.at[side]))
        for i, road_ref in enumerate((speed_ref, wave_ref, jam_ref, share_ref)):
            copies.append(
                pltpu.make_async_copy(
                    road_ref.at[:, at], tile_ref.at[pl.ds(rows + i, 1), :], sem_ref.at[2 + 4 * side + i]
                )
            )
    for d in range(GROUP):
        at = pl.ds(pl.multiple_of(lax.rem(member + d, GROUP) * SLOTS, LANES), SLOTS)
        copies.append(pltpu.make_async_copy(noise_ref.at[:, at], noise_refs[d], sem_ref.at[10 + d]))
    for copy in copies:
        copy.start()
    for copy in copies:
        copy.wait()
    last, first = tile_refs[0][:, LANES - TICKS :], tile_refs[1][:, :TICKS]
    even = lax.rem(place_ref[1], 2) == 0
    near_ref[...] = jnp.where(even, last, first)
    far_ref[...] = jnp.where(even, first, last)


def edges(place, state, road, noise):
    rows = state.shape[0]
    edge = jax.ShapeDtypeStruct((rows + 4, TICKS), jnp.float32)
    piece = jax.ShapeDtypeStruct((rows, SLOTS), jnp.float32)
    return pl.pallas_call(
        edges_kernel,
        out_shape=(edge,) * 2 + (piece,) * GROUP,
        in_specs=[SMEM] + [HBM] * 6,
        out_specs=(VMEM,) * (2 + GROUP),
        scratch_shapes=[pltpu.VMEM((rows + 4, LANES), jnp.float32)] * 2 + [pltpu.SemaphoreType.DMA((10 + GROUP,))],
        compiler_params=room(4),
        name="edges",
    )(place, state, *road, noise)


def forecast_kernel(
    place_ref, state_ref, near_ref, far_ref, speed_ref, wave_ref, jam_ref, share_ref, cells_ref, *refs
):
    fore_refs, obs_refs = refs[:GROUP], refs[GROUP : 2 * GROUP]
    wide_ref, other_ref, side_ref, share_at, cell_ref, sem_ref = refs[2 * GROUP :]
    rows, width = state_ref.shape
    full = width + 2 * LANES
    main = slice(LANES, LANES + width)
    inner = pl.ds(LANES, width)
    roads = [
        pltpu.make_async_copy(ref, side_ref.at[pl.ds(i, 1), inner], sem_ref.at[i])
        for i, ref in enumerate((speed_ref, wave_ref, jam_ref))
    ]
    roads.append(pltpu.make_async_copy(share_ref, share_at, sem_ref.at[3]))
    arrive = pltpu.make_async_copy(state_ref, wide_ref.at[:, inner], sem_ref.at[4])
    fetch = pltpu.make_async_copy(cells_ref, cell_ref, sem_ref.at[5])
    for copy in roads + [arrive, fetch]:
        copy.start()
    member = place_ref[0]
    slab = place_ref[1]
    is_first = slab == 0
    is_last = slab == place_ref[2] - 1
    for copy in roads:
        copy.wait()
    capacity = road_capacity(side_ref[0:1, main], side_ref[1:2, main], side_ref[2:3, main], share_at[...])
    side_ref[3:4, main] = capacity
    edge = jnp.zeros((rows + 4, LANES - TICKS), jnp.float32)
    even = lax.rem(slab, 2) == 0
    low = jnp.concatenate([edge, jnp.where(even, far_ref[...], near_ref[...])], axis=1)
    high = jnp.concatenate([jnp.where(even, near_ref[...], far_ref[...]), edge], axis=1)
    wide_ref[:, :LANES] = low[:rows]
    wide_ref[:, LANES + width :] = high[:rows]
    lane = lax.broadcasted_iota(jnp.int32, (1, LANES), 1)
    for piece, at, inside, beyond in (
        (low, slice(0, LANES), lane >= LANES - TICKS, is_first),
        (high, slice(LANES + width, full), lane < TICKS, is_last),
    ):
        inside = inside & jnp.logical_not(beyond)
        s, w, j, c = [piece[rows + i : rows + i + 1] for i in range(4)]
        s = jnp.where(inside, s, 1.0)
        w = jnp.where(inside, w, 1.0)
        j = jnp.where(inside, j, 1.0)
        c = jnp.where(inside, c, 0.0)
        side_ref[0:1, at] = s
        side_ref[1:2, at] = w
        side_ref[2:3, at] = j
        side_ref[3:4, at] = road_capacity(s, w, j, c)

    @pl.when(is_last)
    def _():
        at = slice(LANES + width, full)
        side_ref[0:1, at] = jnp.zeros((1, LANES), jnp.float32)
        side_ref[2:3, at] = jnp.full((1, LANES), 1000.0, jnp.float32)
        side_ref[3:4, at] = jnp.broadcast_to(capacity[:, width - 1 :], (1, LANES))

    arrive.wait()

    def half(src, dst):
        for g in range(rows // 8):
            at = slice(8 * g, 8 * g + 8)
            x = src[at, :]
            cap = side_ref[3:4, :]
            demand = jnp.minimum(side_ref[0:1, :] * x, cap)
            supply = jnp.minimum(cap, side_ref[1:2, :] * (side_ref[2:3, :] - x))
            flux = jnp.minimum(demand, pltpu.roll(supply, full - 1, 1))
            dst[at, :] = x + pltpu.roll(flux, 1, 1) - flux

    def step(_, carry):
        half(wide_ref, other_ref)
        half(other_ref, wide_ref)
        return carry

    lax.fori_loop(0, TICKS // 2, step, 0)
    starts = [pl.multiple_of(LANES + lax.rem(member + d, GROUP) * CELLS, LANES) for d in range(GROUP)]
    leave = [
        pltpu.make_async_copy(wide_ref.at[:, pl.ds(starts[d], CELLS)], fore_refs[d], sem_ref.at[6 + d])
        for d in range(GROUP)
    ]
    for copy in leave:
        copy.start()
    fetch.wait()
    for d, obs_ref in enumerate(obs_refs):
        b = lax.rem(member + d, GROUP)
        start = starts[d]

        def gather(q, carry):
            cells = cell_ref[pl.ds(b * PER_BLOCK + q, 1), :]
            at_lane = jnp.broadcast_to(cells & (LANES - 1), (8, LANES))
            tile = jnp.broadcast_to(cells >> 7, (8, LANES))
            acc = [jnp.zeros((8, LANES), jnp.float32) for _ in range(rows // 8)]
            for c in range(CELLS // LANES):
                hit = tile == c
                for g in range(rows // 8):
                    piece = wide_ref[8 * g : 8 * g + 8, pl.ds(start + c * LANES, LANES)]
                    acc[g] = jnp.where(hit, jnp.take_along_axis(piece, at_lane, axis=1), acc[g])
            for g in range(rows // 8):
                obs_ref[q, 8 * g : 8 * g + 8, :] = acc[g]
            return carry

        lax.fori_loop(0, PER_BLOCK, gather, 0, unroll=True)
    for copy in leave:
        copy.wait()


def forecast(place, state, near, far, road, cells):
    rows, width = state.shape
    piece = jax.ShapeDtypeStruct((PER_BLOCK, rows, LANES), jnp.float32)
    return pl.pallas_call(
        forecast_kernel,
        out_shape=(jax.ShapeDtypeStruct((rows, CELLS), jnp.float32),) * GROUP + (piece,) * GROUP,
        in_specs=[SMEM, HBM, VMEM, VMEM] + [HBM] * 5,
        out_specs=(HBM,) * GROUP + (VMEM,) * GROUP,
        scratch_shapes=[
            pltpu.VMEM((rows, width + 2 * LANES), jnp.float32),
            pltpu.VMEM((rows, width + 2 * LANES), jnp.float32),
            pltpu.VMEM((8, width + 2 * LANES), jnp.float32),
            pltpu.VMEM((1, width), jnp.float32),
            pltpu.VMEM(cells.shape, jnp.int32),
            pltpu.SemaphoreType.DMA((6 + GROUP,)),
        ],
        compiler_params=room(12),
        name="forecast",
    )(place, state, near, far, *road, cells)


def sums_kernel(*refs):
    place_ref, counts_ref = refs[:2]
    obs_refs, noise_refs = refs[2 : 2 + GROUP], refs[2 + GROUP : 2 + 2 * GROUP]
    value_ref, variance_ref, left_ref, right_ref, sum_ref, count_ref, sem_ref = refs[2 + 2 * GROUP :]
    fetch = pltpu.make_async_copy(counts_ref, count_ref, sem_ref.at[0])
    fetch.start()
    member = place_ref[0]
    rows = noise_refs[0].shape[0]
    for d in range(GROUP):
        at = pl.multiple_of(lax.rem(member - d + GROUP, GROUP) * rows, rows)
        for q in range(PER_BLOCK):
            left_ref[pl.ds(at, rows), q * LANES : (q + 1) * LANES] = obs_refs[d][q]
        right_ref[pl.ds(TALLY + at, rows), :] = noise_refs[d][...]
    fetch.wait()
    count = count_ref[member]
    total_a = jnp.zeros((1, LANES), jnp.float32)
    total_b = jnp.zeros((1, LANES), jnp.float32)
    for q in range(PER_BLOCK):
        at = slice(q * LANES, (q + 1) * LANES)
        x = left_ref[:, at]
        value = value_ref[pl.ds(member * PER_BLOCK + q, 1), :]
        variance = variance_ref[pl.ds(member * PER_BLOCK + q, 1), :]
        mean = jnp.sum(x, axis=0, keepdims=True) / TALLY
        a = x - mean
        slot = lax.broadcasted_iota(jnp.int32, (1, LANES), 1) + q * LANES
        live = (slot < count).astype(jnp.float32)
        weight = live / variance
        misfit = value - mean
        spread = jnp.sum(a * a, axis=0, keepdims=True) / (TALLY - 1)
        total_a += misfit * misfit * weight
        total_b += live * (spread / variance + 1.0)
        left_ref[:, at] = a * weight
        right_ref[:TALLY, at] = a
        right_ref[TALLY:, at] = misfit + jnp.sqrt(variance) * right_ref[TALLY:, at]
    lane = lax.broadcasted_iota(jnp.int32, (1, LANES), 1)
    sum_a = jnp.sum(total_a, axis=1, keepdims=True)
    sum_b = jnp.sum(total_b, axis=1, keepdims=True)
    sums = jnp.where(lane == 0, sum_a, jnp.where(lane == 1, sum_b, 0.0))
    sum_ref[...] = jnp.broadcast_to(sums[None], sum_ref.shape)


def observed_sums(place, count, obs, noise, value, variance, copies):
    rows = noise[0].shape[0]
    return pl.pallas_call(
        sums_kernel,
        out_shape=(
            jax.ShapeDtypeStruct((GROUP * rows, SLOTS), jnp.float32),
            jax.ShapeDtypeStruct((2 * GROUP * rows, SLOTS), jnp.float32),
            jax.ShapeDtypeStruct((copies, 1, LANES), jnp.float32),
        ),
        in_specs=[SMEM, HBM] + [VMEM] * (2 * GROUP + 2),
        out_specs=(VMEM,) * 3,
        scratch_shapes=[pltpu.SMEM((GROUP,), jnp.int32), pltpu.SemaphoreType.DMA((1,))],
        compiler_params=room(6),
        name="observed_sums",
    )(place, count, *obs, *noise, value, variance)


def products_kernel(left_ref, right_ref, pair_ref):
    dims = (((1,), (1,)), ((), ()))
    both = lax.dot_general(
        left_ref[...], right_ref[...], dims, precision=HIGHEST, preferred_element_type=jnp.float32
    )
    pair_ref[0] = both[:, :TALLY]
    pair_ref[1] = both[:, TALLY:]


def products(left, right):
    return pl.pallas_call(
        products_kernel,
        out_shape=PAIR,
        in_specs=[VMEM] * 2,
        out_specs=VMEM,
        compiler_params=room(6),
        name="products",
    )(left, right)


def select_kernel(place_ref, list_ref, near_ref, pair_ref, far_ref, *out_refs):
    member = place_ref[0]
    slab = place_ref[1]
    beside = 1 - 2 * lax.rem(slab, 2)
    for d in range(GROUP):
        target = lax.rem(member + d, GROUP)
        total = None
        for step, ref in ((0, pair_ref), (beside, near_ref), (-beside, far_ref)):
            name = (slab + step) * GROUP + member
            listed = (list_ref[target, 0] == name) | (list_ref[target, 1] == name) | (list_ref[target, 2] == name)
            share = jnp.where(listed, jnp.float32(1.0), jnp.float32(0.0)) * ref[...]
            total = share if total is None else total + share
        out_refs[d][...] = total


def select(place, lists, near, pair, far):
    return pl.pallas_call(
        select_kernel,
        out_shape=(PAIR,) * GROUP,
        in_specs=[SMEM, SMEM] + [VMEM] * 3,
        out_specs=(VMEM,) * GROUP,
        compiler_params=room(6),
        name="select",
    )(place, lists, near, pair, far)


def eliminate(tiles):
    sub = lax.broadcasted_iota(jnp.int32, (8, 2 * TALLY), 0)
    total = len(tiles)
    for k in range(total):
        rows = [jnp.broadcast_to(tiles[k][j : j + 1, :], (8, 2 * TALLY)) for j in range(8)]
        w = {}
        for i in range(8):
            for j in range(i, 8):
                w[i, j] = jnp.broadcast_to(rows[i][:, 8 * k + j : 8 * k + j + 1], (8, LANES))
        for p in range(8):
            inverse = 1.0 / w[p, p]
            line = {i: w[min(i, p), max(i, p)] for i in range(8) if i != p}
            part = {i: line[i] * inverse for i in line}
            for i in line:
                for j in line:
                    if i <= j:
                        w[i, j] = w[i, j] - line[i] * part[j]
            for i in line:
                w[min(i, p), max(i, p)] = part[i]
            w[p, p] = -inverse
        fresh = []
        for i in range(8):
            row = None
            for j in range(8):
                entry = w[min(i, j), max(i, j)]
                term = jnp.concatenate([entry, entry], axis=1) * rows[j]
                row = term if row is None else row + term
            fresh.append(-row)
        for i in range(1, total + 1):
            i = (k + i) % total
            tile = tiles[i]
            if i == k:
                for j in range(8):
                    tile = jnp.where(sub == j, fresh[j], tile)
            else:
                for j in range(8):
                    column = jnp.broadcast_to(tiles[i][:, 8 * k + j : 8 * k + j + 1], (8, LANES))
                    tile = tile - jnp.concatenate([column, column], axis=1) * fresh[j]
            tiles[i] = tile
    return tiles


def update_kernel(place_ref, part0_ref, part1_ref, part2_ref, part3_ref, sums_ref, *refs):
    fore_refs = refs[:GROUP]
    out_ref, state_ref, sem_ref = refs[GROUP:]
    rows = fore_refs[0].shape[0]
    member = place_ref[0]
    arrive = []
    for d in range(GROUP):
        at = pl.multiple_of(lax.rem(member - d + GROUP, GROUP) * rows, rows)
        arrive.append(pltpu.make_async_copy(fore_refs[d], state_ref.at[pl.ds(at, rows), :], sem_ref.at[d]))
    for copy in arrive:
        copy.start()
    sums = jnp.sum(sums_ref[...], axis=0, keepdims=True)
    gram = (part0_ref[0] + part1_ref[0]) + (part2_ref[0] + part3_ref[0])
    cross = (part0_ref[1] + part1_ref[1]) + (part2_ref[1] + part3_ref[1])
    scale = jnp.sqrt(sums[:, 0:1] / sums[:, 1:2])
    row = lax.broadcasted_iota(jnp.int32, (TALLY, TALLY), 0)
    lane = lax.broadcasted_iota(jnp.int32, (TALLY, TALLY), 1)
    eye = jnp.where(row == lane, jnp.float32(TALLY - 1), jnp.float32(0.0))
    both = jnp.concatenate([eye + (scale * scale) * gram, eye + scale * cross], axis=1)
    tiles = eliminate([both[8 * i : 8 * i + 8, :] for i in range(TALLY // 8)])
    mixing = jnp.concatenate([tile[:, TALLY:] for tile in tiles], axis=0) * scale
    for copy in arrive:
        copy.wait()
    state = state_ref[...]
    mean = jnp.sum(state, axis=0, keepdims=True) / TALLY
    anomaly = state - mean
    dims = (((0,), (0,)), ((), ()))
    out = mean + lax.dot_general(mixing, anomaly, dims, precision=HIGHEST, preferred_element_type=jnp.float32)
    for m in range(GROUP):
        out_ref[m] = out[m * rows : (m + 1) * rows, :]


def update(place, parts, sums, fore):
    return pl.pallas_call(
        update_kernel,
        out_shape=jax.ShapeDtypeStruct((GROUP,) + fore[0].shape, jnp.float32),
        in_specs=[SMEM] + [VMEM] * 5 + [HBM] * GROUP,
        out_specs=VMEM,
        scratch_shapes=[pltpu.VMEM((TALLY, CELLS), jnp.float32), pltpu.SemaphoreType.DMA((GROUP,))],
        compiler_params=room(10),
        name="update",
    )(place, *parts, sums, *fore)


def hold(value):
    return pltpu.with_memory_space_constraint(value, pltpu.HBM)


def exchange(pieces):
    moved = {
        d: lax.ppermute(pieces[d], "member", [(i, (i + d) % GROUP) for i in range(GROUP)]) for d in (2, 1, 3)
    }
    return [pieces[0], moved[1], moved[2], moved[3]]


def swap(value, first):
    slabs = lax.axis_size(RB)
    up = [(i, i + 1) for i in range(first, slabs - 1, 2)]
    return lax.ppermute(value, RB, up + [(b, a) for a, b in up])


def body(load, free_speed, wave_speed, jam_density, capacity_share, cell, count, value, variance, noise, lists):
    rows, width = load.shape
    member = lax.axis_index("member")
    slab = lax.axis_index(RB)
    slabs = lax.axis_size(RB)
    place = jnp.stack([member, slab, jnp.int32(slabs)]).astype(jnp.int32)

    road = [hold(v.reshape(1, width)) for v in (free_speed, wave_speed, jam_density, capacity_share)]
    load, noise, count, cells = [hold(v) for v in (load, noise, count, cell.reshape(-1, LANES))]
    near, far, *noises = edges(place, load, road, noise)
    near, far = swap(near, 0), swap(far, 1)
    out = forecast(place, load, near, far, road, cells)
    fore, obs = out[:GROUP], out[GROUP:]
    obs = exchange(obs)
    noises = exchange(noises)
    fore = exchange(fore)

    left, right, sums = observed_sums(
        place, count, obs, noises, value.reshape(-1, LANES), variance.reshape(-1, LANES), GROUP * slabs
    )
    pair = products(left, right)
    near, far = swap(pair, 0), swap(pair, 1)
    near, far, sums = lax.optimization_barrier((near, far, sums))
    sums = lax.all_to_all(sums, ALL, 0, 0).reshape(GROUP * slabs, LANES)
    parts = exchange(select(place, lists, near, pair, far))
    out = update(place, parts, sums, fore)
    out = lax.all_to_all(out, "member", 0, 0)
    return out.transpose(1, 0, 2).reshape(rows, width)


def solution(mesh):
    slab = P(RB)
    in_specs = (P("member", RB),) + (slab,) * 8 + (P("member", RB), P(RB, None))
    return jax.shard_map(body, mesh=mesh, in_specs=in_specs, out_specs=P("member", RB), check_vma=False)
```

```python
import jax
import jax.numpy as jnp
from jax import lax
from jax.experimental import pallas as pl
from jax.experimental.pallas import tpu as pltpu
from jax.sharding import PartitionSpec as P

TALLY = 128
TICKS = 16
CELLS = 2048
SLOTS = 768
LANES = 128
GROUP = 4
BATCH = 6
SPAN = LANES + 2 * TICKS
PER_BLOCK = SLOTS // LANES
RB = ("region", "block")
ALL = ("member", "region", "block")
HIGHEST = lax.Precision.HIGHEST
VMEM = pl.BlockSpec(memory_space=pltpu.VMEM)
SMEM = pl.BlockSpec(memory_space=pltpu.SMEM)
HBM = pl.BlockSpec(memory_space=pltpu.HBM)


def room(mib):
    return pltpu.CompilerParams(vmem_limit_bytes=mib << 20)


PAIR = jax.ShapeDtypeStruct((2, TALLY, TALLY), jnp.float32)


def road_capacity(free_speed, wave_speed, jam_density, capacity_share):
    return capacity_share * free_speed * wave_speed * jam_density / (free_speed + wave_speed)


def edges_kernel(place_ref, state_ref, speed_ref, wave_ref, jam_ref, share_ref, noise_ref, *refs):
    near_ref, far_ref = refs[:2]
    noise_refs = refs[2 : 2 + GROUP]
    tile_refs = refs[2 + GROUP : 4 + GROUP]
    sem_ref = refs[4 + GROUP]
    rows, width = state_ref.shape
    member = place_ref[0]
    copies = []
    for side, tile_ref in enumerate(tile_refs):
        at = pl.ds((1 - side) * (width - LANES), LANES)
        copies.append(pltpu.make_async_copy(state_ref.at[:, at], tile_ref.at[pl.ds(0, rows), :], sem_ref.at[side]))
        for i, road_ref in enumerate((speed_ref, wave_ref, jam_ref, share_ref)):
            copies.append(
                pltpu.make_async_copy(
                    road_ref.at[:, at], tile_ref.at[pl.ds(rows + i, 1), :], sem_ref.at[2 + 4 * side + i]
                )
            )
    for d in range(GROUP):
        at = pl.ds(pl.multiple_of(lax.rem(member + d, GROUP) * SLOTS, LANES), SLOTS)
        copies.append(pltpu.make_async_copy(noise_ref.at[:, at], noise_refs[d], sem_ref.at[10 + d]))
    for copy in copies:
        copy.start()
    for copy in copies:
        copy.wait()
    last, first = tile_refs[0][:, LANES - TICKS :], tile_refs[1][:, :TICKS]
    even = lax.rem(place_ref[1], 2) == 0
    near_ref[...] = jnp.where(even, last, first)
    far_ref[...] = jnp.where(even, first, last)


def edges(place, state, road, noise):
    rows = state.shape[0]
    edge = jax.ShapeDtypeStruct((rows + 4, TICKS), jnp.float32)
    piece = jax.ShapeDtypeStruct((rows, SLOTS), jnp.float32)
    return pl.pallas_call(
        edges_kernel,
        out_shape=(edge,) * 2 + (piece,) * GROUP,
        in_specs=[SMEM] + [HBM] * 6,
        out_specs=(VMEM,) * (2 + GROUP),
        scratch_shapes=[pltpu.VMEM((rows + 4, LANES), jnp.float32)] * 2 + [pltpu.SemaphoreType.DMA((10 + GROUP,))],
        compiler_params=room(4),
        name="edges",
    )(place, state, *road, noise)


def advance(wide_ref, side_ref, tiles_ref, strip_ref, road_ref, here_ref, there_ref):
    rows = wide_ref.shape[0]
    count = wide_ref.shape[1] // LANES
    inner = count - 2
    pairs = rows // 2
    right = SPAN - TICKS
    lane = lax.broadcasted_iota(jnp.int32, (LANES, LANES), 1)
    for i in range(4):
        for v in range(count):
            strip_ref[7 + v : 8 + v, :] = side_ref[i : i + 1, v * LANES : (v + 1) * LANES]
        own, before, after = [strip_ref[n : n + inner, :] for n in (8, 7, 9)]
        beside = jnp.where(lane[:inner] >= inner, before, after)
        own = jnp.concatenate([own, own], axis=0).T
        beside = jnp.concatenate([beside, beside], axis=0).T
        for s in range(8):
            road_ref[i, pl.ds(TICKS * 8 + s, LANES, stride=8), :] = own
            road_ref[i, pl.ds(s, TICKS, stride=8), :] = beside[LANES - TICKS :]
            road_ref[i, pl.ds(right * 8 + s, TICKS, stride=8), :] = beside[:TICKS]
    for g in range(rows // 8):
        for v in range(count):
            at = (g * count + v) * 8
            tiles_ref[at : at + 8, :] = wide_ref[8 * g : 8 * g + 8, v * LANES : (v + 1) * LANES]

    def member_rows(p, h, shift):
        r = p + pairs * h
        return pl.ds((r // 8 * count + 1 + shift) * 8 + r % 8, inner, stride=8)

    def pair_rows(p, shift):
        return jnp.concatenate([tiles_ref[member_rows(p, h, shift), :] for h in (0, 1)], axis=0)

    for p in range(pairs):
        beside = jnp.where(lane >= inner, pair_rows(p, -1), pair_rows(p, 1)).T
        here_ref[pl.ds(TICKS * pairs + p, LANES, stride=pairs), :] = pair_rows(p, 0).T
        here_ref[pl.ds(p, TICKS, stride=pairs), :] = beside[LANES - TICKS :]
        here_ref[pl.ds(right * pairs + p, TICKS, stride=pairs), :] = beside[:TICKS]

    def half(src, dst, first):
        for at in range(first, SPAN - first, BATCH):
            n = min(BATCH, SPAN - first - at)
            x = src[(at - 1) * pairs : (at + n + 1) * pairs, :].reshape(n + 2, pairs // 8, 8, LANES)
            speed, wave, jam, cap = [
                road_ref[i, (at - 1) * 8 : (at + n + 1) * 8, :].reshape(n + 2, 1, 8, LANES) for i in range(4)
            ]
            demand = jnp.minimum(speed[:-1] * x[:-1], cap[:-1])
            supply = jnp.minimum(cap[1:], wave[1:] * (jam[1:] - x[1:]))
            flux = jnp.minimum(demand, supply)
            dst[at * pairs : (at + n) * pairs, :] = (x[1:-1] + flux[:-1] - flux[1:]).reshape(n * pairs, LANES)

    for first in (1, 1 + TICKS // 2):

        def step(_, carry):
            half(here_ref, there_ref, first)
            half(there_ref, here_ref, first)
            return carry

        lax.fori_loop(0, TICKS // 4, step, 0)
    for p in range(pairs):
        done = here_ref[pl.ds(TICKS * pairs + p, LANES, stride=pairs), :].T
        for h in (0, 1):
            tiles_ref[member_rows(p, h, 0), :] = done[inner * h : inner * (h + 1)]
    for g in range(rows // 8):
        for v in range(1, count - 1):
            at = (g * count + v) * 8
            wide_ref[8 * g : 8 * g + 8, v * LANES : (v + 1) * LANES] = tiles_ref[at : at + 8, :]


def forecast_kernel(
    place_ref, state_ref, near_ref, far_ref, speed_ref, wave_ref, jam_ref, share_ref, cells_ref, *refs
):
    fore_refs, obs_refs = refs[:GROUP], refs[GROUP : 2 * GROUP]
    wide_ref, side_ref, share_at, cell_ref, sem_ref = refs[2 * GROUP : 2 * GROUP + 5]
    tiles_ref, strip_ref, road_ref, here_ref, there_ref = refs[2 * GROUP + 5 :]
    rows, width = state_ref.shape
    full = width + 2 * LANES
    main = slice(LANES, LANES + width)
    inner = pl.ds(LANES, width)
    roads = [
        pltpu.make_async_copy(ref, side_ref.at[pl.ds(i, 1), inner], sem_ref.at[i])
        for i, ref in enumerate((speed_ref, wave_ref, jam_ref))
    ]
    roads.append(pltpu.make_async_copy(share_ref, share_at, sem_ref.at[3]))
    arrive = pltpu.make_async_copy(state_ref, wide_ref.at[:, inner], sem_ref.at[4])
    fetch = pltpu.make_async_copy(cells_ref, cell_ref, sem_ref.at[5])
    for copy in roads + [arrive, fetch]:
        copy.start()
    member = place_ref[0]
    slab = place_ref[1]
    is_first = slab == 0
    is_last = slab == place_ref[2] - 1
    for copy in roads:
        copy.wait()
    capacity = road_capacity(side_ref[0:1, main], side_ref[1:2, main], side_ref[2:3, main], share_at[...])
    side_ref[3:4, main] = capacity
    edge = jnp.zeros((rows + 4, LANES - TICKS), jnp.float32)
    even = lax.rem(slab, 2) == 0
    low = jnp.concatenate([edge, jnp.where(even, far_ref[...], near_ref[...])], axis=1)
    high = jnp.concatenate([jnp.where(even, near_ref[...], far_ref[...]), edge], axis=1)
    wide_ref[:, :LANES] = low[:rows]
    wide_ref[:, LANES + width :] = high[:rows]
    lane = lax.broadcasted_iota(jnp.int32, (1, LANES), 1)
    for piece, at, inside, beyond in (
        (low, slice(0, LANES), lane >= LANES - TICKS, is_first),
        (high, slice(LANES + width, full), lane < TICKS, is_last),
    ):
        inside = inside & jnp.logical_not(beyond)
        s, w, j, c = [piece[rows + i : rows + i + 1] for i in range(4)]
        s = jnp.where(inside, s, 1.0)
        w = jnp.where(inside, w, 1.0)
        j = jnp.where(inside, j, 1.0)
        c = jnp.where(inside, c, 0.0)
        side_ref[0:1, at] = s
        side_ref[1:2, at] = w
        side_ref[2:3, at] = j
        side_ref[3:4, at] = road_capacity(s, w, j, c)

    @pl.when(is_last)
    def _():
        at = slice(LANES + width, full)
        side_ref[0:1, at] = jnp.zeros((1, LANES), jnp.float32)
        side_ref[2:3, at] = jnp.full((1, LANES), 1000.0, jnp.float32)
        side_ref[3:4, at] = jnp.broadcast_to(capacity[:, width - 1 :], (1, LANES))

    arrive.wait()

    advance(wide_ref, side_ref, tiles_ref, strip_ref, road_ref, here_ref, there_ref)
    starts = [pl.multiple_of(LANES + lax.rem(member + d, GROUP) * CELLS, LANES) for d in range(GROUP)]
    leave = [
        pltpu.make_async_copy(wide_ref.at[:, pl.ds(starts[d], CELLS)], fore_refs[d], sem_ref.at[6 + d])
        for d in range(GROUP)
    ]
    for copy in leave:
        copy.start()
    fetch.wait()
    for d, obs_ref in enumerate(obs_refs):
        b = lax.rem(member + d, GROUP)
        start = starts[d]

        def gather(q, carry):
            cells = cell_ref[pl.ds(b * PER_BLOCK + q, 1), :]
            at_lane = jnp.broadcast_to(cells & (LANES - 1), (8, LANES))
            tile = jnp.broadcast_to(cells >> 7, (8, LANES))
            acc = [jnp.zeros((8, LANES), jnp.float32) for _ in range(rows // 8)]
            for c in range(CELLS // LANES):
                hit = tile == c
                for g in range(rows // 8):
                    piece = wide_ref[8 * g : 8 * g + 8, pl.ds(start + c * LANES, LANES)]
                    acc[g] = jnp.where(hit, jnp.take_along_axis(piece, at_lane, axis=1), acc[g])
            for g in range(rows // 8):
                obs_ref[q, 8 * g : 8 * g + 8, :] = acc[g]
            return carry

        lax.fori_loop(0, PER_BLOCK, gather, 0, unroll=True)
    for copy in leave:
        copy.wait()


def forecast(place, state, near, far, road, cells):
    rows, width = state.shape
    piece = jax.ShapeDtypeStruct((PER_BLOCK, rows, LANES), jnp.float32)
    return pl.pallas_call(
        forecast_kernel,
        out_shape=(jax.ShapeDtypeStruct((rows, CELLS), jnp.float32),) * GROUP + (piece,) * GROUP,
        in_specs=[SMEM, HBM, VMEM, VMEM] + [HBM] * 5,
        out_specs=(HBM,) * GROUP + (VMEM,) * GROUP,
        scratch_shapes=[
            pltpu.VMEM((rows, width + 2 * LANES), jnp.float32),
            pltpu.VMEM((8, width + 2 * LANES), jnp.float32),
            pltpu.VMEM((1, width), jnp.float32),
            pltpu.VMEM(cells.shape, jnp.int32),
            pltpu.SemaphoreType.DMA((6 + GROUP,)),
            pltpu.VMEM((rows * (width // LANES + 2), LANES), jnp.float32),
            pltpu.VMEM((width // LANES + 16, LANES), jnp.float32),
            pltpu.VMEM((4, SPAN * 8, LANES), jnp.float32),
            pltpu.VMEM((SPAN * rows // 2, LANES), jnp.float32),
            pltpu.VMEM((SPAN * rows // 2, LANES), jnp.float32),
        ],
        compiler_params=room(14),
        name="forecast",
    )(place, state, near, far, *road, cells)


def sums_kernel(*refs):
    place_ref, counts_ref = refs[:2]
    obs_refs, noise_refs = refs[2 : 2 + GROUP], refs[2 + GROUP : 2 + 2 * GROUP]
    value_ref, variance_ref, left_ref, right_ref, sum_ref, count_ref, sem_ref = refs[2 + 2 * GROUP :]
    fetch = pltpu.make_async_copy(counts_ref, count_ref, sem_ref.at[0])
    fetch.start()
    member = place_ref[0]
    rows = noise_refs[0].shape[0]
    for d in range(GROUP):
        at = pl.multiple_of(lax.rem(member - d + GROUP, GROUP) * rows, rows)
        for q in range(PER_BLOCK):
            left_ref[pl.ds(at, rows), q * LANES : (q + 1) * LANES] = obs_refs[d][q]
        right_ref[pl.ds(TALLY + at, rows), :] = noise_refs[d][...]
    fetch.wait()
    count = count_ref[member]
    total_a = jnp.zeros((1, LANES), jnp.float32)
    total_b = jnp.zeros((1, LANES), jnp.float32)
    for q in range(PER_BLOCK):
        at = slice(q * LANES, (q + 1) * LANES)
        x = left_ref[:, at]
        value = value_ref[pl.ds(member * PER_BLOCK + q, 1), :]
        variance = variance_ref[pl.ds(member * PER_BLOCK + q, 1), :]
        mean = jnp.sum(x, axis=0, keepdims=True) / TALLY
        a = x - mean
        slot = lax.broadcasted_iota(jnp.int32, (1, LANES), 1) + q * LANES
        live = (slot < count).astype(jnp.float32)
        weight = live / variance
        misfit = value - mean
        spread = jnp.sum(a * a, axis=0, keepdims=True) / (TALLY - 1)
        total_a += misfit * misfit * weight
        total_b += live * (spread / variance + 1.0)
        left_ref[:, at] = a * weight
        right_ref[:TALLY, at] = a
        right_ref[TALLY:, at] = misfit + jnp.sqrt(variance) * right_ref[TALLY:, at]
    lane = lax.broadcasted_iota(jnp.int32, (1, LANES), 1)
    sum_a = jnp.sum(total_a, axis=1, keepdims=True)
    sum_b = jnp.sum(total_b, axis=1, keepdims=True)
    sums = jnp.where(lane == 0, sum_a, jnp.where(lane == 1, sum_b, 0.0))
    sum_ref[...] = jnp.broadcast_to(sums[None], sum_ref.shape)


def observed_sums(place, count, obs, noise, value, variance, copies):
    rows = noise[0].shape[0]
    return pl.pallas_call(
        sums_kernel,
        out_shape=(
            jax.ShapeDtypeStruct((GROUP * rows, SLOTS), jnp.float32),
            jax.ShapeDtypeStruct((2 * GROUP * rows, SLOTS), jnp.float32),
            jax.ShapeDtypeStruct((copies, 1, LANES), jnp.float32),
        ),
        in_specs=[SMEM, HBM] + [VMEM] * (2 * GROUP + 2),
        out_specs=(VMEM,) * 3,
        scratch_shapes=[pltpu.SMEM((GROUP,), jnp.int32), pltpu.SemaphoreType.DMA((1,))],
        compiler_params=room(6),
        name="observed_sums",
    )(place, count, *obs, *noise, value, variance)


def products_kernel(left_ref, right_ref, pair_ref):
    dims = (((1,), (1,)), ((), ()))
    both = lax.dot_general(
        left_ref[...], right_ref[...], dims, precision=HIGHEST, preferred_element_type=jnp.float32
    )
    pair_ref[0] = both[:, :TALLY]
    pair_ref[1] = both[:, TALLY:]


def products(left, right):
    return pl.pallas_call(
        products_kernel,
        out_shape=PAIR,
        in_specs=[VMEM] * 2,
        out_specs=VMEM,
        compiler_params=room(6),
        name="products",
    )(left, right)


def select_kernel(place_ref, list_ref, near_ref, pair_ref, far_ref, *out_refs):
    member = place_ref[0]
    slab = place_ref[1]
    beside = 1 - 2 * lax.rem(slab, 2)
    for d in range(GROUP):
        target = lax.rem(member + d, GROUP)
        total = None
        for step, ref in ((0, pair_ref), (beside, near_ref), (-beside, far_ref)):
            name = (slab + step) * GROUP + member
            listed = (list_ref[target, 0] == name) | (list_ref[target, 1] == name) | (list_ref[target, 2] == name)
            share = jnp.where(listed, jnp.float32(1.0), jnp.float32(0.0)) * ref[...]
            total = share if total is None else total + share
        out_refs[d][...] = total


def select(place, lists, near, pair, far):
    return pl.pallas_call(
        select_kernel,
        out_shape=(PAIR,) * GROUP,
        in_specs=[SMEM, SMEM] + [VMEM] * 3,
        out_specs=(VMEM,) * GROUP,
        compiler_params=room(6),
        name="select",
    )(place, lists, near, pair, far)


def eliminate(tiles):
    sub = lax.broadcasted_iota(jnp.int32, (8, 2 * TALLY), 0)
    total = len(tiles)
    for k in range(total):
        rows = [jnp.broadcast_to(tiles[k][j : j + 1, :], (8, 2 * TALLY)) for j in range(8)]
        w = {}
        for i in range(8):
            for j in range(i, 8):
                w[i, j] = jnp.broadcast_to(rows[i][:, 8 * k + j : 8 * k + j + 1], (8, LANES))
        for p in range(8):
            inverse = 1.0 / w[p, p]
            line = {i: w[min(i, p), max(i, p)] for i in range(8) if i != p}
            part = {i: line[i] * inverse for i in line}
            for i in line:
                for j in line:
                    if i <= j:
                        w[i, j] = w[i, j] - line[i] * part[j]
            for i in line:
                w[min(i, p), max(i, p)] = part[i]
            w[p, p] = -inverse
        fresh = []
        for i in range(8):
            row = None
            for j in range(8):
                entry = w[min(i, j), max(i, j)]
                term = jnp.concatenate([entry, entry], axis=1) * rows[j]
                row = term if row is None else row + term
            fresh.append(-row)
        for i in range(1, total + 1):
            i = (k + i) % total
            tile = tiles[i]
            if i == k:
                for j in range(8):
                    tile = jnp.where(sub == j, fresh[j], tile)
            else:
                for j in range(8):
                    column = jnp.broadcast_to(tiles[i][:, 8 * k + j : 8 * k + j + 1], (8, LANES))
                    tile = tile - jnp.concatenate([column, column], axis=1) * fresh[j]
            tiles[i] = tile
    return tiles


def update_kernel(place_ref, part0_ref, part1_ref, part2_ref, part3_ref, sums_ref, *refs):
    fore_refs = refs[:GROUP]
    out_refs = refs[GROUP : 2 * GROUP]
    state_ref, sem_ref = refs[2 * GROUP :]
    rows = fore_refs[0].shape[0]
    member = place_ref[0]
    arrive = []
    for d in range(GROUP):
        at = pl.multiple_of(lax.rem(member - d + GROUP, GROUP) * rows, rows)
        arrive.append(pltpu.make_async_copy(fore_refs[d], state_ref.at[pl.ds(at, rows), :], sem_ref.at[d]))
    for copy in arrive:
        copy.start()
    sums = jnp.sum(sums_ref[...], axis=0, keepdims=True)
    gram = (part0_ref[0] + part1_ref[0]) + (part2_ref[0] + part3_ref[0])
    cross = (part0_ref[1] + part1_ref[1]) + (part2_ref[1] + part3_ref[1])
    scale = jnp.sqrt(sums[:, 0:1] / sums[:, 1:2])
    row = lax.broadcasted_iota(jnp.int32, (TALLY, TALLY), 0)
    lane = lax.broadcasted_iota(jnp.int32, (TALLY, TALLY), 1)
    eye = jnp.where(row == lane, jnp.float32(TALLY - 1), jnp.float32(0.0))
    both = jnp.concatenate([eye + (scale * scale) * gram, eye + scale * cross], axis=1)
    tiles = eliminate([both[8 * i : 8 * i + 8, :] for i in range(TALLY // 8)])
    mixing = jnp.concatenate([tile[:, TALLY:] for tile in tiles], axis=0) * scale
    for copy in arrive:
        copy.wait()
    state = state_ref[...]
    mean = jnp.sum(state, axis=0, keepdims=True) / TALLY
    anomaly = state - mean
    dims = (((0,), (0,)), ((), ()))
    state_ref[...] = mean + lax.dot_general(
        mixing, anomaly, dims, precision=HIGHEST, preferred_element_type=jnp.float32
    )
    for d in range(GROUP):
        at = pl.multiple_of(lax.rem(member + d, GROUP) * rows, rows)
        out_refs[d][...] = state_ref[pl.ds(at, rows), :]


def update(place, parts, sums, fore):
    return pl.pallas_call(
        update_kernel,
        out_shape=(jax.ShapeDtypeStruct(fore[0].shape, jnp.float32),) * GROUP,
        in_specs=[SMEM] + [VMEM] * 5 + [HBM] * GROUP,
        out_specs=(VMEM,) * GROUP,
        scratch_shapes=[pltpu.VMEM((TALLY, CELLS), jnp.float32), pltpu.SemaphoreType.DMA((GROUP,))],
        compiler_params=room(10),
        name="update",
    )(place, *parts, sums, *fore)


def assemble_kernel(place_ref, *refs):
    out_ref, sem_ref = refs[GROUP:]
    copies = []
    for d in range(GROUP):
        b = lax.rem(place_ref[0] - d + GROUP, GROUP)
        at = pl.ds(pl.multiple_of(b * CELLS, LANES), CELLS)
        copies.append(pltpu.make_async_copy(refs[d], out_ref.at[:, at], sem_ref.at[d]))
    for copy in copies:
        copy.start()
    for copy in copies:
        copy.wait()


def assemble(place, pieces):
    rows = pieces[0].shape[0]
    return pl.pallas_call(
        assemble_kernel,
        out_shape=jax.ShapeDtypeStruct((rows, GROUP * CELLS), jnp.float32),
        in_specs=[SMEM] + [HBM] * GROUP,
        out_specs=HBM,
        scratch_shapes=[pltpu.SemaphoreType.DMA((GROUP,))],
        compiler_params=room(4),
        name="assemble",
    )(place, *pieces)


def hold(value):
    return pltpu.with_memory_space_constraint(value, pltpu.HBM)


def exchange(pieces):
    moved = {
        d: lax.ppermute(pieces[d], "member", [(i, (i + d) % GROUP) for i in range(GROUP)]) for d in (2, 1, 3)
    }
    return [pieces[0], moved[1], moved[2], moved[3]]


def swap(value, first):
    slabs = lax.axis_size(RB)
    up = [(i, i + 1) for i in range(first, slabs - 1, 2)]
    return lax.ppermute(value, RB, up + [(b, a) for a, b in up])


def body(load, free_speed, wave_speed, jam_density, capacity_share, cell, count, value, variance, noise, lists):
    rows, width = load.shape
    member = lax.axis_index("member")
    slab = lax.axis_index(RB)
    slabs = lax.axis_size(RB)
    place = jnp.stack([member, slab, jnp.int32(slabs)]).astype(jnp.int32)

    road = [hold(v.reshape(1, width)) for v in (free_speed, wave_speed, jam_density, capacity_share)]
    load, noise, count, cells = [hold(v) for v in (load, noise, count, cell.reshape(-1, LANES))]
    near, far, *noises = edges(place, load, road, noise)
    near, far = swap(near, 0), swap(far, 1)
    out = forecast(place, load, near, far, road, cells)
    fore, obs = out[:GROUP], out[GROUP:]
    obs = exchange(obs)
    noises = exchange(noises)
    fore = exchange(fore)

    left, right, sums = observed_sums(
        place, count, obs, noises, value.reshape(-1, LANES), variance.reshape(-1, LANES), GROUP * slabs
    )
    pair = products(left, right)
    near, far = swap(pair, 0), swap(pair, 1)
    near, far, sums = lax.optimization_barrier((near, far, sums))
    sums = lax.all_to_all(sums, ALL, 0, 0).reshape(GROUP * slabs, LANES)
    parts = exchange(select(place, lists, near, pair, far))
    return assemble(place, exchange(update(place, parts, sums, fore)))


def solution(mesh):
    slab = P(RB)
    in_specs = (P("member", RB),) + (slab,) * 8 + (P("member", RB), P(RB, None))
    return jax.shard_map(body, mesh=mesh, in_specs=in_specs, out_specs=P("member", RB), check_vma=False)
```

```python
import jax
import jax.numpy as jnp
from jax import lax
from jax.experimental import pallas as pl
from jax.experimental.pallas import tpu as pltpu
from jax.sharding import PartitionSpec as P

TALLY = 128
TICKS = 16
CELLS = 2048
SLOTS = 768
LANES = 128
GROUP = 4
BATCH = 6
SPAN = LANES + 2 * TICKS
PER_BLOCK = SLOTS // LANES
RB = ("region", "block")
ALL = ("member", "region", "block")
HIGHEST = lax.Precision.HIGHEST
VMEM = pl.BlockSpec(memory_space=pltpu.VMEM)
SMEM = pl.BlockSpec(memory_space=pltpu.SMEM)
HBM = pl.BlockSpec(memory_space=pltpu.HBM)


def room(mib):
    return pltpu.CompilerParams(vmem_limit_bytes=mib << 20)


PAIR = jax.ShapeDtypeStruct((2, TALLY, TALLY), jnp.float32)


def road_capacity(free_speed, wave_speed, jam_density, capacity_share):
    return capacity_share * free_speed * wave_speed * jam_density / (free_speed + wave_speed)


def edges_kernel(place_ref, state_ref, speed_ref, wave_ref, jam_ref, share_ref, noise_ref, *refs):
    near_ref, far_ref = refs[:2]
    noise_refs = refs[2 : 2 + GROUP]
    tile_refs = refs[2 + GROUP : 4 + GROUP]
    sem_ref = refs[4 + GROUP]
    rows, width = state_ref.shape
    member = place_ref[0]
    copies = []
    for side, tile_ref in enumerate(tile_refs):
        at = pl.ds((1 - side) * (width - LANES), LANES)
        copies.append(pltpu.make_async_copy(state_ref.at[:, at], tile_ref.at[pl.ds(0, rows), :], sem_ref.at[side]))
        for i, road_ref in enumerate((speed_ref, wave_ref, jam_ref, share_ref)):
            copies.append(
                pltpu.make_async_copy(
                    road_ref.at[:, at], tile_ref.at[pl.ds(rows + i, 1), :], sem_ref.at[2 + 4 * side + i]
                )
            )
    for d in range(GROUP):
        at = pl.ds(pl.multiple_of(lax.rem(member + d, GROUP) * SLOTS, LANES), SLOTS)
        copies.append(pltpu.make_async_copy(noise_ref.at[:, at], noise_refs[d], sem_ref.at[10 + d]))
    for copy in copies:
        copy.start()
    for copy in copies:
        copy.wait()
    last, first = tile_refs[0][:, LANES - TICKS :], tile_refs[1][:, :TICKS]
    even = lax.rem(place_ref[1], 2) == 0
    near_ref[...] = jnp.where(even, last, first)
    far_ref[...] = jnp.where(even, first, last)


def edges(place, state, road, noise):
    rows = state.shape[0]
    edge = jax.ShapeDtypeStruct((rows + 4, TICKS), jnp.float32)
    piece = jax.ShapeDtypeStruct((rows, SLOTS), jnp.float32)
    return pl.pallas_call(
        edges_kernel,
        out_shape=(edge,) * 2 + (piece,) * GROUP,
        in_specs=[SMEM] + [HBM] * 6,
        out_specs=(VMEM,) * (2 + GROUP),
        scratch_shapes=[pltpu.VMEM((rows + 4, LANES), jnp.float32)] * 2 + [pltpu.SemaphoreType.DMA((10 + GROUP,))],
        compiler_params=room(4),
        name="edges",
    )(place, state, *road, noise)


def advance(wide_ref, side_ref, tiles_ref, strip_ref, road_ref, here_ref, there_ref):
    rows = wide_ref.shape[0]
    count = wide_ref.shape[1] // LANES
    inner = count - 2
    pairs = rows // 2
    right = SPAN - TICKS
    lane = lax.broadcasted_iota(jnp.int32, (LANES, LANES), 1)
    for i in range(4):
        for v in range(count):
            strip_ref[7 + v : 8 + v, :] = side_ref[i : i + 1, v * LANES : (v + 1) * LANES]
        own, before, after = [strip_ref[n : n + inner, :] for n in (8, 7, 9)]
        beside = jnp.where(lane[:inner] >= inner, before, after)
        own = jnp.concatenate([own, own], axis=0).T
        beside = jnp.concatenate([beside, beside], axis=0).T
        for s in range(8):
            road_ref[i, pl.ds(TICKS * 8 + s, LANES, stride=8), :] = own
            road_ref[i, pl.ds(s, TICKS, stride=8), :] = beside[LANES - TICKS :]
            road_ref[i, pl.ds(right * 8 + s, TICKS, stride=8), :] = beside[:TICKS]
    for g in range(rows // 8):
        for v in range(count):
            at = (g * count + v) * 8
            tiles_ref[at : at + 8, :] = wide_ref[8 * g : 8 * g + 8, v * LANES : (v + 1) * LANES]

    def member_rows(p, h, shift):
        r = p + pairs * h
        return pl.ds((r // 8 * count + 1 + shift) * 8 + r % 8, inner, stride=8)

    def pair_rows(p, shift):
        return jnp.concatenate([tiles_ref[member_rows(p, h, shift), :] for h in (0, 1)], axis=0)

    for p in range(pairs):
        beside = jnp.where(lane >= inner, pair_rows(p, -1), pair_rows(p, 1)).T
        here_ref[pl.ds(TICKS * pairs + p, LANES, stride=pairs), :] = pair_rows(p, 0).T
        here_ref[pl.ds(p, TICKS, stride=pairs), :] = beside[LANES - TICKS :]
        here_ref[pl.ds(right * pairs + p, TICKS, stride=pairs), :] = beside[:TICKS]

    def half(src, dst, first):
        for at in range(first, SPAN - first, BATCH):
            n = min(BATCH, SPAN - first - at)
            x = src[(at - 1) * pairs : (at + n + 1) * pairs, :].reshape(n + 2, pairs // 8, 8, LANES)
            speed, wave, jam, cap = [
                road_ref[i, (at - 1) * 8 : (at + n + 1) * 8, :].reshape(n + 2, 1, 8, LANES) for i in range(4)
            ]
            demand = jnp.minimum(speed[:-1] * x[:-1], cap[:-1])
            supply = jnp.minimum(cap[1:], wave[1:] * (jam[1:] - x[1:]))
            flux = jnp.minimum(demand, supply)
            dst[at * pairs : (at + n) * pairs, :] = (x[1:-1] + flux[:-1] - flux[1:]).reshape(n * pairs, LANES)

    for first in (1, 1 + TICKS // 2):

        def step(_, carry):
            half(here_ref, there_ref, first)
            half(there_ref, here_ref, first)
            return carry

        lax.fori_loop(0, TICKS // 4, step, 0)
    for p in range(pairs):
        done = here_ref[pl.ds(TICKS * pairs + p, LANES, stride=pairs), :].T
        for h in (0, 1):
            tiles_ref[member_rows(p, h, 0), :] = done[inner * h : inner * (h + 1)]
    for g in range(rows // 8):
        for v in range(1, count - 1):
            at = (g * count + v) * 8
            wide_ref[8 * g : 8 * g + 8, v * LANES : (v + 1) * LANES] = tiles_ref[at : at + 8, :]


def forecast_kernel(
    place_ref, state_ref, near_ref, far_ref, speed_ref, wave_ref, jam_ref, share_ref, cells_ref, *refs
):
    fore_refs, obs_refs = refs[:GROUP], refs[GROUP : 2 * GROUP]
    wide_ref, side_ref, share_at, cell_ref, sem_ref = refs[2 * GROUP : 2 * GROUP + 5]
    tiles_ref, strip_ref, road_ref, here_ref, there_ref = refs[2 * GROUP + 5 :]
    rows, width = state_ref.shape
    full = width + 2 * LANES
    main = slice(LANES, LANES + width)
    inner = pl.ds(LANES, width)
    roads = [
        pltpu.make_async_copy(ref, side_ref.at[pl.ds(i, 1), inner], sem_ref.at[i])
        for i, ref in enumerate((speed_ref, wave_ref, jam_ref))
    ]
    roads.append(pltpu.make_async_copy(share_ref, share_at, sem_ref.at[3]))
    arrive = pltpu.make_async_copy(state_ref, wide_ref.at[:, inner], sem_ref.at[4])
    fetch = pltpu.make_async_copy(cells_ref, cell_ref, sem_ref.at[5])
    for copy in roads + [arrive, fetch]:
        copy.start()
    member = place_ref[0]
    slab = place_ref[1]
    is_first = slab == 0
    is_last = slab == place_ref[2] - 1
    for copy in roads:
        copy.wait()
    capacity = road_capacity(side_ref[0:1, main], side_ref[1:2, main], side_ref[2:3, main], share_at[...])
    side_ref[3:4, main] = capacity
    edge = jnp.zeros((rows + 4, LANES - TICKS), jnp.float32)
    even = lax.rem(slab, 2) == 0
    low = jnp.concatenate([edge, jnp.where(even, far_ref[...], near_ref[...])], axis=1)
    high = jnp.concatenate([jnp.where(even, near_ref[...], far_ref[...]), edge], axis=1)
    wide_ref[:, :LANES] = low[:rows]
    wide_ref[:, LANES + width :] = high[:rows]
    lane = lax.broadcasted_iota(jnp.int32, (1, LANES), 1)
    for piece, at, inside, beyond in (
        (low, slice(0, LANES), lane >= LANES - TICKS, is_first),
        (high, slice(LANES + width, full), lane < TICKS, is_last),
    ):
        inside = inside & jnp.logical_not(beyond)
        s, w, j, c = [piece[rows + i : rows + i + 1] for i in range(4)]
        s = jnp.where(inside, s, 1.0)
        w = jnp.where(inside, w, 1.0)
        j = jnp.where(inside, j, 1.0)
        c = jnp.where(inside, c, 0.0)
        side_ref[0:1, at] = s
        side_ref[1:2, at] = w
        side_ref[2:3, at] = j
        side_ref[3:4, at] = road_capacity(s, w, j, c)

    @pl.when(is_last)
    def _():
        at = slice(LANES + width, full)
        side_ref[0:1, at] = jnp.zeros((1, LANES), jnp.float32)
        side_ref[2:3, at] = jnp.full((1, LANES), 1000.0, jnp.float32)
        side_ref[3:4, at] = jnp.broadcast_to(capacity[:, width - 1 :], (1, LANES))

    arrive.wait()

    advance(wide_ref, side_ref, tiles_ref, strip_ref, road_ref, here_ref, there_ref)
    starts = [pl.multiple_of(LANES + lax.rem(member + d, GROUP) * CELLS, LANES) for d in range(GROUP)]
    leave = [
        pltpu.make_async_copy(wide_ref.at[:, pl.ds(starts[d], CELLS)], fore_refs[d], sem_ref.at[6 + d])
        for d in range(GROUP)
    ]
    for copy in leave:
        copy.start()
    fetch.wait()
    for d, obs_ref in enumerate(obs_refs):
        b = lax.rem(member + d, GROUP)
        start = starts[d]

        def gather(q, carry):
            cells = cell_ref[pl.ds(b * PER_BLOCK + q, 1), :]
            at_lane = jnp.broadcast_to(cells & (LANES - 1), (8, LANES))
            tile = jnp.broadcast_to(cells >> 7, (8, LANES))
            acc = [jnp.zeros((8, LANES), jnp.float32) for _ in range(rows // 8)]
            for c in range(CELLS // LANES):
                hit = tile == c
                for g in range(rows // 8):
                    piece = wide_ref[8 * g : 8 * g + 8, pl.ds(start + c * LANES, LANES)]
                    acc[g] = jnp.where(hit, jnp.take_along_axis(piece, at_lane, axis=1), acc[g])
            for g in range(rows // 8):
                obs_ref[q, 8 * g : 8 * g + 8, :] = acc[g]
            return carry

        lax.fori_loop(0, PER_BLOCK, gather, 0, unroll=True)
    for copy in leave:
        copy.wait()


def forecast(place, state, near, far, road, cells):
    rows, width = state.shape
    piece = jax.ShapeDtypeStruct((PER_BLOCK, rows, LANES), jnp.float32)
    return pl.pallas_call(
        forecast_kernel,
        out_shape=(jax.ShapeDtypeStruct((rows, CELLS), jnp.float32),) * GROUP + (piece,) * GROUP,
        in_specs=[SMEM, HBM, VMEM, VMEM] + [HBM] * 5,
        out_specs=(HBM,) * GROUP + (VMEM,) * GROUP,
        scratch_shapes=[
            pltpu.VMEM((rows, width + 2 * LANES), jnp.float32),
            pltpu.VMEM((8, width + 2 * LANES), jnp.float32),
            pltpu.VMEM((1, width), jnp.float32),
            pltpu.VMEM(cells.shape, jnp.int32),
            pltpu.SemaphoreType.DMA((6 + GROUP,)),
            pltpu.VMEM((rows * (width // LANES + 2), LANES), jnp.float32),
            pltpu.VMEM((width // LANES + 16, LANES), jnp.float32),
            pltpu.VMEM((4, SPAN * 8, LANES), jnp.float32),
            pltpu.VMEM((SPAN * rows // 2, LANES), jnp.float32),
            pltpu.VMEM((SPAN * rows // 2, LANES), jnp.float32),
        ],
        compiler_params=room(14),
        name="forecast",
    )(place, state, near, far, *road, cells)


def sums_kernel(*refs):
    place_ref, counts_ref = refs[:2]
    obs_refs, noise_refs = refs[2 : 2 + GROUP], refs[2 + GROUP : 2 + 2 * GROUP]
    value_ref, variance_ref, left_ref, right_ref, sum_ref, count_ref, sem_ref = refs[2 + 2 * GROUP :]
    fetch = pltpu.make_async_copy(counts_ref, count_ref, sem_ref.at[0])
    fetch.start()
    member = place_ref[0]
    rows = noise_refs[0].shape[0]
    for d in range(GROUP):
        at = pl.multiple_of(lax.rem(member - d + GROUP, GROUP) * rows, rows)
        for q in range(PER_BLOCK):
            left_ref[pl.ds(at, rows), q * LANES : (q + 1) * LANES] = obs_refs[d][q]
        right_ref[pl.ds(TALLY + at, rows), :] = noise_refs[d][...]
    fetch.wait()
    count = count_ref[member]
    total_a = jnp.zeros((1, LANES), jnp.float32)
    total_b = jnp.zeros((1, LANES), jnp.float32)
    for q in range(PER_BLOCK):
        at = slice(q * LANES, (q + 1) * LANES)
        x = left_ref[:, at]
        value = value_ref[pl.ds(member * PER_BLOCK + q, 1), :]
        variance = variance_ref[pl.ds(member * PER_BLOCK + q, 1), :]
        mean = jnp.sum(x, axis=0, keepdims=True) / TALLY
        a = x - mean
        slot = lax.broadcasted_iota(jnp.int32, (1, LANES), 1) + q * LANES
        live = (slot < count).astype(jnp.float32)
        weight = live / variance
        misfit = value - mean
        spread = jnp.sum(a * a, axis=0, keepdims=True) / (TALLY - 1)
        total_a += misfit * misfit * weight
        total_b += live * (spread / variance + 1.0)
        left_ref[:, at] = a * weight
        right_ref[:TALLY, at] = a
        right_ref[TALLY:, at] = misfit + jnp.sqrt(variance) * right_ref[TALLY:, at]
    lane = lax.broadcasted_iota(jnp.int32, (1, LANES), 1)
    sum_a = jnp.sum(total_a, axis=1, keepdims=True)
    sum_b = jnp.sum(total_b, axis=1, keepdims=True)
    sums = jnp.where(lane == 0, sum_a, jnp.where(lane == 1, sum_b, 0.0))
    sum_ref[...] = jnp.broadcast_to(sums, sum_ref.shape)


def observed_sums(place, count, obs, noise, value, variance, copies):
    rows = noise[0].shape[0]
    return pl.pallas_call(
        sums_kernel,
        out_shape=(
            jax.ShapeDtypeStruct((GROUP * rows, SLOTS), jnp.float32),
            jax.ShapeDtypeStruct((2 * GROUP * rows, SLOTS), jnp.float32),
            jax.ShapeDtypeStruct((copies, LANES), jnp.float32),
        ),
        in_specs=[SMEM, HBM] + [VMEM] * (2 * GROUP + 2),
        out_specs=(VMEM,) * 3,
        scratch_shapes=[pltpu.SMEM((GROUP,), jnp.int32), pltpu.SemaphoreType.DMA((1,))],
        compiler_params=room(6),
        name="observed_sums",
    )(place, count, *obs, *noise, value, variance)


def products_kernel(left_ref, right_ref, pair_ref):
    dims = (((1,), (1,)), ((), ()))
    both = lax.dot_general(
        left_ref[...], right_ref[...], dims, precision=HIGHEST, preferred_element_type=jnp.float32
    )
    pair_ref[0] = both[:, :TALLY]
    pair_ref[1] = both[:, TALLY:]


def products(left, right):
    return pl.pallas_call(
        products_kernel,
        out_shape=PAIR,
        in_specs=[VMEM] * 2,
        out_specs=VMEM,
        compiler_params=room(6),
        name="products",
    )(left, right)


def select_kernel(place_ref, list_ref, near_ref, pair_ref, far_ref, *out_refs):
    member = place_ref[0]
    slab = place_ref[1]
    beside = 1 - 2 * lax.rem(slab, 2)
    for d in range(GROUP):
        target = lax.rem(member + d, GROUP)
        total = None
        for step, ref in ((0, pair_ref), (beside, near_ref), (-beside, far_ref)):
            name = (slab + step) * GROUP + member
            listed = (list_ref[target, 0] == name) | (list_ref[target, 1] == name) | (list_ref[target, 2] == name)
            share = jnp.where(listed, jnp.float32(1.0), jnp.float32(0.0)) * ref[...]
            total = share if total is None else total + share
        out_refs[d][...] = total


def select(place, lists, near, pair, far):
    return pl.pallas_call(
        select_kernel,
        out_shape=(PAIR,) * GROUP,
        in_specs=[SMEM, SMEM] + [VMEM] * 3,
        out_specs=(VMEM,) * GROUP,
        compiler_params=room(6),
        name="select",
    )(place, lists, near, pair, far)


def eliminate(tiles):
    sub = lax.broadcasted_iota(jnp.int32, (8, 2 * TALLY), 0)
    total = len(tiles)
    for k in range(total):
        rows = [jnp.broadcast_to(tiles[k][j : j + 1, :], (8, 2 * TALLY)) for j in range(8)]
        w = {}
        for i in range(8):
            for j in range(i, 8):
                w[i, j] = jnp.broadcast_to(rows[i][:, 8 * k + j : 8 * k + j + 1], (8, LANES))
        for p in range(8):
            inverse = 1.0 / w[p, p]
            line = {i: w[min(i, p), max(i, p)] for i in range(8) if i != p}
            part = {i: line[i] * inverse for i in line}
            for i in line:
                for j in line:
                    if i <= j:
                        w[i, j] = w[i, j] - line[i] * part[j]
            for i in line:
                w[min(i, p), max(i, p)] = part[i]
            w[p, p] = -inverse
        fresh = []
        for i in range(8):
            row = None
            for j in range(8):
                entry = w[min(i, j), max(i, j)]
                term = jnp.concatenate([entry, entry], axis=1) * rows[j]
                row = term if row is None else row + term
            fresh.append(-row)
        for i in range(1, total + 1):
            i = (k + i) % total
            tile = tiles[i]
            if i == k:
                for j in range(8):
                    tile = jnp.where(sub == j, fresh[j], tile)
            else:
                for j in range(8):
                    column = jnp.broadcast_to(tiles[i][:, 8 * k + j : 8 * k + j + 1], (8, LANES))
                    tile = tile - jnp.concatenate([column, column], axis=1) * fresh[j]
            tiles[i] = tile
    return tiles


def halves(value):
    high = value.astype(jnp.bfloat16)
    return high, (value - high.astype(jnp.float32)).astype(jnp.bfloat16)


def update_kernel(place_ref, part0_ref, part1_ref, part2_ref, part3_ref, sums_ref, *refs):
    fore_refs = refs[:GROUP]
    out_refs = refs[GROUP : 2 * GROUP]
    state_ref, sem_ref = refs[2 * GROUP :]
    rows = fore_refs[0].shape[0]
    member = place_ref[0]
    arrive = []
    for d in range(GROUP):
        at = pl.multiple_of(lax.rem(member - d + GROUP, GROUP) * rows, rows)
        arrive.append(pltpu.make_async_copy(fore_refs[d], state_ref.at[pl.ds(at, rows), :], sem_ref.at[d]))
    for copy in arrive:
        copy.start()
    sums = jnp.sum(sums_ref[...], axis=0, keepdims=True)
    gram = (part0_ref[0] + part1_ref[0]) + (part2_ref[0] + part3_ref[0])
    cross = (part0_ref[1] + part1_ref[1]) + (part2_ref[1] + part3_ref[1])
    scale = jnp.sqrt(sums[:, 0:1] / sums[:, 1:2])
    row = lax.broadcasted_iota(jnp.int32, (TALLY, TALLY), 0)
    lane = lax.broadcasted_iota(jnp.int32, (TALLY, TALLY), 1)
    eye = jnp.where(row == lane, jnp.float32(TALLY - 1), jnp.float32(0.0))
    both = jnp.concatenate([eye + (scale * scale) * gram, eye + scale * cross], axis=1)
    tiles = eliminate([both[8 * i : 8 * i + 8, :] for i in range(TALLY // 8)])
    mixing = jnp.concatenate([tile[:, TALLY:] for tile in tiles], axis=0) * scale
    for copy in arrive:
        copy.wait()
    state = state_ref[...]
    mean = jnp.sum(state, axis=0, keepdims=True) / TALLY
    anomaly = state - mean
    dims = (((0,), (0,)), ((), ()))
    mix_high, mix_low = halves(mixing)
    high, low = halves(anomaly)
    first = lax.dot_general(mix_high, low, dims, preferred_element_type=jnp.float32)
    first += lax.dot_general(mix_low, high, dims, preferred_element_type=jnp.float32)
    state_ref[...] = mean + (first + lax.dot_general(mix_high, high, dims, preferred_element_type=jnp.float32))
    for d in range(GROUP):
        at = pl.multiple_of(lax.rem(member + d, GROUP) * rows, rows)
        out_refs[d][...] = state_ref[pl.ds(at, rows), :]


def update(place, parts, sums, fore):
    return pl.pallas_call(
        update_kernel,
        out_shape=(jax.ShapeDtypeStruct(fore[0].shape, jnp.float32),) * GROUP,
        in_specs=[SMEM] + [VMEM] * 5 + [HBM] * GROUP,
        out_specs=(VMEM,) * GROUP,
        scratch_shapes=[pltpu.VMEM((TALLY, CELLS), jnp.float32), pltpu.SemaphoreType.DMA((GROUP,))],
        compiler_params=room(10),
        name="update",
    )(place, *parts, sums, *fore)


def assemble_kernel(place_ref, *refs):
    out_ref, sem_ref = refs[GROUP:]
    copies = []
    for d in range(GROUP):
        b = lax.rem(place_ref[0] - d + GROUP, GROUP)
        at = pl.ds(pl.multiple_of(b * CELLS, LANES), CELLS)
        copies.append(pltpu.make_async_copy(refs[d], out_ref.at[:, at], sem_ref.at[d]))
    for copy in copies:
        copy.start()
    for copy in copies:
        copy.wait()


def assemble(place, pieces):
    rows = pieces[0].shape[0]
    return pl.pallas_call(
        assemble_kernel,
        out_shape=jax.ShapeDtypeStruct((rows, GROUP * CELLS), jnp.float32),
        in_specs=[SMEM] + [HBM] * GROUP,
        out_specs=HBM,
        scratch_shapes=[pltpu.SemaphoreType.DMA((GROUP,))],
        compiler_params=room(4),
        name="assemble",
    )(place, *pieces)


def hold(value):
    return pltpu.with_memory_space_constraint(value, pltpu.HBM)


def exchange(pieces):
    moved = {
        d: lax.ppermute(pieces[d], "member", [(i, (i + d) % GROUP) for i in range(GROUP)]) for d in (2, 1, 3)
    }
    return [pieces[0], moved[1], moved[2], moved[3]]


def swap(value, first):
    slabs = lax.axis_size(RB)
    up = [(i, i + 1) for i in range(first, slabs - 1, 2)]
    return lax.ppermute(value, RB, up + [(b, a) for a, b in up])


def body(load, free_speed, wave_speed, jam_density, capacity_share, cell, count, value, variance, noise, lists):
    rows, width = load.shape
    member = lax.axis_index("member")
    slab = lax.axis_index(RB)
    slabs = lax.axis_size(RB)
    place = jnp.stack([member, slab, jnp.int32(slabs)]).astype(jnp.int32)

    road = [hold(v.reshape(1, width)) for v in (free_speed, wave_speed, jam_density, capacity_share)]
    load, noise, count, cells = [hold(v) for v in (load, noise, count, cell.reshape(-1, LANES))]
    near, far, *noises = edges(place, load, road, noise)
    near, far = swap(near, 0), swap(far, 1)
    out = forecast(place, load, near, far, road, cells)
    fore, obs = out[:GROUP], out[GROUP:]
    obs = exchange(obs)
    noises = exchange(noises)
    fore = exchange(fore)

    left, right, sums = observed_sums(
        place, count, obs, noises, value.reshape(-1, LANES), variance.reshape(-1, LANES), GROUP * slabs
    )
    pair = products(left, right)
    near, far = swap(pair, 0), swap(pair, 1)
    near, far, sums = lax.optimization_barrier((near, far, sums))
    sums = lax.all_to_all(sums[:, None], ALL, 0, 0).reshape(GROUP * slabs, LANES)
    parts = exchange(select(place, lists, near, pair, far))
    return assemble(place, exchange(update(place, parts, sums, fore)))


def solution(mesh):
    slab = P(RB)
    in_specs = (P("member", RB),) + (slab,) * 8 + (P("member", RB), P(RB, None))
    return jax.shard_map(body, mesh=mesh, in_specs=in_specs, out_specs=P("member", RB), check_vma=False)
```
